32 devices in a mesh: ctx: 8 (over y, x, core), head: 4 (over z).
Axes of the slice: x: 2, y: 2, z: 4, core: 2. Of those that a mesh axis runs over, the one named last changes fastest.
Arguments:
- inputs: bfloat16 [4096, 2048], P('ctx'), may hold values from -6 to 6
- w_query: bfloat16 [2048, 2048], P(None, 'head'), may hold values from -0.125 to 0.125
- w_key: bfloat16 [2048, 2048], P(None, 'head'), may hold values from -0.125 to 0.125
- w_value: bfloat16 [2048, 4096], P(None, 'head'), may hold values from -0.125 to 0.125
- w_gate_out: bfloat16 [2048, 4096], P(None, 'head'), may hold values from -0.125 to 0.125
- conv_query: float32 [4, 2048], P(None, 'head'), may hold values from -3 to 3
- conv_key: float32 [4, 2048], P(None, 'head'), may hold values from -3 to 3
- conv_value: float32 [4, 4096], P(None, 'head'), may hold values from -3 to 3
- decay_log: float32 [32, 4096], P('head', 'ctx'), may hold values from -1 to 0, as said below
- write_rate: float32 [32, 4096], P('head', 'ctx'), may hold values from 0 to 1, as said below
- w_out: bfloat16 [4096, 2048], P('head'), may hold values from -0.09375 to 0.09375
Outputs:
- mixed: bfloat16 [4096, 2048], P(('ctx', 'head'))
The draws below stay inside these ranges and needn't reach their ends.
Inputs may be any that keep to these rules, and one draw needn't show every extreme that they name: `decay_log`: Negative. `write_rate`: Positive.
All inputs are finite; a program needn't handle non-finite values.
Results may differ from the reference program's by a relative error of at most 0.015.
Values may be sent and summed in bfloat16 or wider, within the bound.
No kernel may reach another device: no remote copies, remote signals or barrier semaphores. Data moves between devices by JAX's collectives and lax.ppermute only.
A program may use at most 128 MiB of HBM per device.

```python
import math
import jax
import jax.numpy as jnp
from jax import lax

D = 2048
KEYH = 16
VALUE_HEAD_COUNT = 32
HD = 128
CONV = 4
GROUP = 64
TOK_DEV = 512
SEQUENCE_TOKENS = 4096


def head_plan(key):
    common = jax.random.fold_in(key, 11)
    shuffled = jax.random.permutation(common, VALUE_HEAD_COUNT)
    quick_count = VALUE_HEAD_COUNT // 2
    return shuffled < quick_count


def draw_inputs(key, part):
    subkeys = jax.random.split(jax.random.fold_in(key, 53), 2)
    shared_row = jnp.clip(jax.random.normal(subkeys[0], (1, D), jnp.float32), -5.5, 5.5)
    noise_rows = jnp.clip(jax.random.normal(subkeys[1], (SEQUENCE_TOKENS, D), jnp.float32), -5.5, 5.5)
    mixed_rows = 0.75 * shared_row + 0.3 * noise_rows
    return mixed_rows.astype(jnp.bfloat16)


def draw_decay_log(key, part):
    quick_heads = head_plan(key)
    subkeys = jax.random.split(jax.random.fold_in(key, 23), 6)
    fast_rate = jnp.exp(jax.random.uniform(subkeys[0], (VALUE_HEAD_COUNT, 1), jnp.float32, math.log(1.0 / 50.0), math.log(1.0 / 30.0)))
    slow_rate = jnp.exp(jax.random.uniform(subkeys[1], (VALUE_HEAD_COUNT, 1), jnp.float32, math.log(0.05), math.log(0.3))) / SEQUENCE_TOKENS
    baseline_rate = jnp.where(quick_heads[:, None], fast_rate, slow_rate)
    shard_factor = jnp.exp(jax.random.uniform(subkeys[2], (VALUE_HEAD_COUNT, SEQUENCE_TOKENS // TOK_DEV), jnp.float32, math.log(0.5), math.log(2.0)))
    shard_factor = jnp.repeat(shard_factor, TOK_DEV, axis=1)
    random_noise = jax.random.uniform(subkeys[3], (VALUE_HEAD_COUNT, SEQUENCE_TOKENS), jnp.float32, 0.5, 1.5)
    spike_position = jax.random.randint(subkeys[4], (VALUE_HEAD_COUNT, 2, 1), 0, SEQUENCE_TOKENS)
    token_positions = jnp.arange(SEQUENCE_TOKENS, dtype=jnp.int32)[None, None, :]
    spike_applied = jnp.any(spike_position == token_positions, axis=1)
    spike_depth = jax.random.uniform(subkeys[5], (VALUE_HEAD_COUNT, 1), jnp.float32, math.log(0.55), math.log(0.8))
    return -(baseline_rate * shard_factor * random_noise) + jnp.where(spike_applied, spike_depth, 0.0)


def draw_write_rate(key, part):
    quick_heads = head_plan(key)
    subkeys = jax.random.split(jax.random.fold_in(key, 37), 4)
    fast_rate = jnp.exp(jax.random.uniform(subkeys[0], (VALUE_HEAD_COUNT, 1), jnp.float32, math.log(0.3), math.log(0.9)))
    first_rate = jnp.exp(jax.random.uniform(subkeys[1], (VALUE_HEAD_COUNT, 1), jnp.float32, math.log(0.2), math.log(0.8)))
    later_rate = jnp.exp(jax.random.uniform(subkeys[2], (VALUE_HEAD_COUNT, 1), jnp.float32, math.log(0.2), math.log(1.0))) / SEQUENCE_TOKENS
    token_positions = jnp.arange(SEQUENCE_TOKENS, dtype=jnp.int32)[None, :]
    slow_rate = jnp.where(token_positions < TOK_DEV, first_rate, later_rate)
    baseline_rate = jnp.where(quick_heads[:, None], fast_rate, slow_rate)
    random_noise = jax.random.uniform(subkeys[3], (VALUE_HEAD_COUNT, SEQUENCE_TOKENS), jnp.float32, 0.7, 1.1)
    return baseline_rate * random_noise


def shard_levels(stream_key, extent, cuts, smallest, high):
    def one(axis_at, parts):
        draws = jax.random.uniform(jax.random.fold_in(jax.random.fold_in(stream_key, 6), axis_at), (parts,), jnp.float32, smallest / len(cuts), high / len(cuts))
        return jnp.repeat(jnp.exp(draws), extent[axis_at] // parts).reshape((-1,) + (1,) * (len(extent) - axis_at - 1))

    factor_of = one(*cuts[0])
    for cut in cuts[1:]:
        factor_of = factor_of * one(*cut)
    return factor_of


def normal_values(own_key, dims, scale, reach, cuts=(), kind=jnp.bfloat16):
    array = jax.random.normal(own_key, dims, jnp.float32) * scale
    if len(cuts) > 0:
        array = shard_levels(own_key, dims, cuts, -0.22, 0.18) * array
    return jnp.clip(array, min=-reach, max=reach).astype(kind)


def setup_inputs(seed: int = 0) -> dict:
    seeds = jax.random.split(jax.random.key(seed), 12)
    return {
        "inputs": draw_inputs(jax.random.fold_in(seeds[11], 71), 0),
        "w_query": normal_values(seeds[1], (D, KEYH * HD), D ** -0.5, 0.125, ((1, 4),)),
        "w_key": normal_values(seeds[2], (D, KEYH * HD), D ** -0.5, 0.125, ((1, 4),)),
        "w_value": normal_values(seeds[3], (D, VALUE_HEAD_COUNT * HD), D ** -0.5, 0.125, ((1, 4),)),
        "w_gate_out": normal_values(seeds[4], (D, VALUE_HEAD_COUNT * HD), D ** -0.5, 0.125, ((1, 4),)),
        "conv_query": normal_values(seeds[5], (CONV, KEYH * HD), CONV ** -0.5, 3.0, ((1, 4),), jnp.float32),
        "conv_key": normal_values(seeds[6], (CONV, KEYH * HD), CONV ** -0.5, 3.0, ((1, 4),), jnp.float32),
        "conv_value": normal_values(seeds[7], (CONV, VALUE_HEAD_COUNT * HD), CONV ** -0.5, 3.0, ((1, 4),), jnp.float32),
        "decay_log": draw_decay_log(jax.random.fold_in(seeds[11], 71), 0),
        "write_rate": draw_write_rate(jax.random.fold_in(seeds[11], 71), 0),
        "w_out": normal_values(seeds[10], (VALUE_HEAD_COUNT * HD, D), (VALUE_HEAD_COUNT * HD) ** -0.5, 0.09375, ((0, 4),)),
    }


highest = lax.Precision.HIGHEST

def causal_conv(projected, conv_rims, weights):
    kernel_len = weights.shape[0]
    row_count = projected.shape[0]
    padded = jnp.concatenate([conv_rims, projected], axis=0).astype(jnp.float32)
    summed = weights[0] * padded[0:row_count]
    for offset in range(1, kernel_len):
        summed = summed + weights[offset] * padded[offset:offset + row_count]
    return jax.nn.silu(summed)

def unit_rows(values, factor):
    return values * lax.rsqrt(lax.optimization_barrier(jnp.sum(values * values, axis=-1, keepdims=True)) + 1e-06) * factor

def head_inputs(proj_query, proj_key, proj_value, conv_query, conv_key, conv_value, rims_query, rims_key, rims_value, head_dim):
    row_count = proj_query.shape[0]
    key_heads = proj_query.shape[1] // head_dim
    value_heads = proj_value.shape[1] // head_dim
    ratio_heads = value_heads // key_heads
    conv_q = causal_conv(proj_query, rims_query, conv_query).reshape(row_count, key_heads, head_dim)
    conv_k = causal_conv(proj_key, rims_key, conv_key).reshape(row_count, key_heads, head_dim)
    conv_v = causal_conv(proj_value, rims_value, conv_value).reshape(row_count, value_heads, head_dim)
    queries = unit_rows(conv_q, head_dim ** (-0.5))
    keys_all = unit_rows(conv_k, 1.0)
    queries = jnp.repeat(queries, ratio_heads, axis=1)
    keys_all = jnp.repeat(keys_all, ratio_heads, axis=1)
    return (queries, keys_all, conv_v)

def to_groups(arrays, group_len):
    row_count, heads_count, feat = arrays.shape
    return arrays.reshape(row_count // group_len, group_len, heads_count, feat).transpose(0, 2, 1, 3)

def gates_to_groups(arrays, group_len):
    heads_count, row_count = arrays.shape
    return arrays.reshape(heads_count, row_count // group_len, group_len).transpose(1, 0, 2)

def group_pieces(query_blk, key_blk, value_blk, decay_blk, write_blk):
    group_len = decay_blk.shape[-1]
    key_len = key_blk.shape[-1]
    cumulative = jnp.cumsum(decay_blk, axis=-1)
    row_ids = lax.broadcasted_iota(jnp.int32, (group_len, group_len), 0)
    col_ids = lax.broadcasted_iota(jnp.int32, (group_len, group_len), 1)
    differ = cumulative[:, :, None] - cumulative[:, None, :]
    decay_mat = jnp.where(row_ids >= col_ids, jnp.exp(jnp.minimum(differ, 0.0)), 0.0)
    key_inner = jnp.einsum('hcd,hed->hce', key_blk, key_blk, precision=highest)
    strict_low = jnp.where(row_ids > col_ids, write_blk[:, :, None] * key_inner * decay_mat, 0.0)
    system = strict_low + jnp.eye(group_len, dtype=jnp.float32)
    scaled = jnp.exp(cumulative)
    right_side = jnp.concatenate([key_blk * (write_blk * scaled)[:, :, None], value_blk * write_blk[:, :, None]], axis=-1)
    solved = lax.linalg.triangular_solve(system, right_side, left_side=True, lower=True, unit_diagonal=True)
    wy_keys = solved[..., :key_len]
    wy_values = solved[..., key_len:]
    scores = jnp.einsum('hcd,hed->hce', query_blk, key_blk, precision=highest) * decay_mat
    q_eff = query_blk * scaled[:, :, None] - jnp.einsum('hce,hed->hcd', scores, wy_keys, precision=highest)
    group_end = cumulative[:, -1]
    k_eff = key_blk * jnp.exp(group_end[:, None] - cumulative)[:, :, None]
    carry_decay = jnp.exp(group_end)
    local_out = jnp.einsum('hce,hef->hcf', scores, wy_values, precision=highest)
    local_state = jnp.einsum('hcd,hcf->hdf', k_eff, wy_values, precision=highest)
    return (q_eff, k_eff, wy_keys, carry_decay, local_out, local_state)

def group_apply(pieces, state_now):
    q_eff, k_eff, wy_keys, carry_decay, local_out, local_state = pieces
    out_blk = local_out + jnp.einsum('hcd,hdf->hcf', q_eff, state_now, precision=highest)
    removed = jnp.einsum('hcd,hdf->hcf', wy_keys, state_now, precision=highest)
    state_next = carry_decay[:, None, None] * state_now + local_state - jnp.einsum('hcd,hcf->hdf', k_eff, removed, precision=highest)
    return (out_blk, state_next)

def gated_norm(attended, gate_in):
    row_count = attended.shape[0]
    gating = gate_in.astype(jnp.float32).reshape(attended.shape)
    scaled = attended * lax.rsqrt(lax.optimization_barrier(jnp.mean(attended * attended, axis=-1, keepdims=True)) + 1e-06)
    return (scaled * jax.nn.silu(gating)).astype(jnp.bfloat16).reshape(row_count, -1)

def reference(inputs, w_query, w_key, w_value, w_gate_out, conv_query, conv_key, conv_value, decay_log, write_rate, w_out):
    proj_query = jnp.dot(inputs.astype(jnp.float32), w_query.astype(jnp.float32), preferred_element_type=jnp.float32).astype(jnp.bfloat16)
    proj_key = jnp.dot(inputs.astype(jnp.float32), w_key.astype(jnp.float32), preferred_element_type=jnp.float32).astype(jnp.bfloat16)
    proj_value = jnp.dot(inputs.astype(jnp.float32), w_value.astype(jnp.float32), preferred_element_type=jnp.float32).astype(jnp.bfloat16)
    gate_in = jnp.dot(inputs.astype(jnp.float32), w_gate_out.astype(jnp.float32), preferred_element_type=jnp.float32).astype(jnp.bfloat16)
    rims_query = jnp.zeros((CONV - 1, proj_query.shape[1]), jnp.bfloat16)
    rims_key = jnp.zeros((CONV - 1, proj_key.shape[1]), jnp.bfloat16)
    rims_value = jnp.zeros((CONV - 1, proj_value.shape[1]), jnp.bfloat16)
    queries, keys_all, values_all = head_inputs(proj_query, proj_key, proj_value, conv_query, conv_key, conv_value, rims_query, rims_key, rims_value, HD)
    blocks = (to_groups(queries, GROUP), to_groups(keys_all, GROUP), to_groups(values_all, GROUP), gates_to_groups(decay_log, GROUP), gates_to_groups(write_rate, GROUP))

    def advance(state_now, block_set):
        pieces = group_pieces(*block_set)
        out_blk, state_next = group_apply(pieces, state_now)
        return (state_next, out_blk)
    start_state = jnp.zeros((VALUE_HEAD_COUNT, HD, HD), jnp.float32)
    final_state, outs_all = lax.scan(advance, start_state, blocks)
    attended = outs_all.transpose(0, 2, 1, 3).reshape(SEQUENCE_TOKENS, VALUE_HEAD_COUNT, HD)
    normed = gated_norm(attended, gate_in)
    return jnp.dot(normed.astype(jnp.float32), w_out.astype(jnp.float32), preferred_element_type=jnp.float32).astype(jnp.bfloat16)
```

```python
import functools

import jax
import jax.numpy as jnp
from jax import lax
from jax.experimental import pallas as pl
from jax.experimental.pallas import tpu as pltpu
from jax.sharding import PartitionSpec as P

HD = 128
CHUNK = 128
RIM = 16
BF = jnp.bfloat16
F32 = jnp.float32
EXACT = lax.Precision.HIGHEST


def mm(left, right):
    return jnp.dot(left.astype(BF), right.astype(BF), preferred_element_type=F32)


def mm_nt(left, right):
    return lax.dot_general(
        left.astype(BF), right.astype(BF), (((1,), (1,)), ((), ())), preferred_element_type=F32
    )


def silu(values):
    return values / (1.0 + jnp.exp(-values))


def unit_rows(values, factor):
    return values * (lax.rsqrt(jnp.sum(values * values, axis=-1, keepdims=True) + 1e-06) * factor)


def stage_rows(stage, rims_ref, rows_ref):
    stage[0:8] = rims_ref[RIM - 8 : RIM].astype(F32)
    stage[8:] = rows_ref[...].astype(F32)


def conv_chunk(stage, taps, chunk):
    taps_len = taps.shape[0]
    start = 8 - (taps_len - 1) + chunk * CHUNK
    total = taps[0:1] * stage[start : start + CHUNK]
    for offset in range(1, taps_len):
        total = total + taps[offset : offset + 1] * stage[start + offset : start + offset + CHUNK]
    return silu(total)


def grid_ids():
    row_ids = lax.broadcasted_iota(jnp.int32, (CHUNK, CHUNK), 0)
    col_ids = lax.broadcasted_iota(jnp.int32, (CHUNK, CHUNK), 1)
    return row_ids, col_ids


def cumulated(decay):
    row_ids, col_ids = grid_ids()
    lower = jnp.where(row_ids >= col_ids, 1.0, 0.0)
    dims = (((1,), (1,)), ((), ()))
    as_rows = lax.dot_general(decay, lower, dims, precision=EXACT, preferred_element_type=F32)
    as_cols = lax.dot_general(lower, decay, dims, precision=EXACT, preferred_element_type=F32)
    return as_rows, as_cols


def inverted(systems):
    row_ids, col_ids = grid_ids()
    same = row_ids // 2 == col_ids // 2
    eye = jnp.where(row_ids == col_ids, 1.0, 0.0)
    inverses = [eye - jnp.where(same, system, 0.0) for system in systems]
    size = 2
    while size < CHUNK:
        cross = (row_ids // (2 * size) == col_ids // (2 * size)) & (
            row_ids // size != col_ids // size
        )
        links = [jnp.where(cross, system, 0.0).astype(BF) for system in systems]
        halves = [inverse.astype(BF) for inverse in inverses]
        if size < 8:
            inner = [mm(link, half) for link, half in zip(links, halves)]
            outer = [mm(half, part) for half, part in zip(halves, inner)]
            inverses = [inverse - part for inverse, part in zip(inverses, outer)]
        else:
            starts = range(size, CHUNK, 2 * size)
            odd = [
                jnp.concatenate([inverse[s : s + size] for s in starts], axis=0)
                for inverse in inverses
            ]
            inner = [mm(part, link) for part, link in zip(odd, links)]
            outer = [mm(part, half) for part, half in zip(inner, halves)]
            odd = [part - update for part, update in zip(odd, outer)]
            inverses = [
                jnp.concatenate(
                    [
                        piece
                        for at, s in enumerate(starts)
                        for piece in (
                            inverse[s - size : s],
                            part[at * size : (at + 1) * size],
                        )
                    ],
                    axis=0,
                )
                for inverse, part in zip(inverses, odd)
            ]
        size *= 2
    return inverses


def local_kernel(
    ratio,
    chunks,
    keys_ref,
    values_ref,
    rims_k_ref,
    rims_v_ref,
    taps_k_ref,
    taps_v_ref,
    decay_ref,
    write_ref,
    keys_out,
    wy_out,
    starts_out,
    map_out,
    stage_k,
    stage_v,
):
    row_ids, col_ids = grid_ids()
    stage_rows(stage_k, rims_k_ref, keys_ref)
    stage_rows(stage_v, rims_v_ref, values_ref)
    decay_rows, decay_cols = cumulated(decay_ref[0])
    write_cols = lax.dot_general(
        jnp.where(row_ids == col_ids, 1.0, 0.0),
        write_ref[0],
        (((1,), (1,)), ((), ())),
        precision=EXACT,
        preferred_element_type=F32,
    )
    taps_k = taps_k_ref[...]
    taps_v = taps_v_ref[...]
    keys = []
    flipped = []
    values = []
    inner = []
    for chunk in range(chunks):
        key = unit_rows(conv_chunk(stage_k, taps_k, chunk), 1.0)
        keys_out[chunk * CHUNK : (chunk + 1) * CHUNK] = key.astype(BF)
        keys.append(key)
        flipped.append(key.T)
        inner.append(mm(key, flipped[-1]))
        values.append(conv_chunk(stage_v, taps_v, chunk))
    units = [(head, chunk) for head in range(ratio) for chunk in range(chunks)]
    systems = []
    for head, chunk in units:
        at = head * chunks + chunk
        fading = jnp.exp(
            jnp.minimum(decay_cols[:, at : at + 1] - decay_rows[at : at + 1], 0.0)
        )
        systems.append(
            jnp.where(
                row_ids > col_ids, write_cols[:, at : at + 1] * inner[chunk] * fading, 0.0
            )
        )
    inverses = inverted(systems)
    maps = []
    for (head, chunk), inverse in zip(units, inverses):
        at = head * chunks + chunk
        col = decay_cols[:, at : at + 1]
        write = write_cols[:, at : at + 1]
        value = values[chunk][:, head * HD : (head + 1) * HD]
        right = jnp.concatenate([keys[chunk] * (write * jnp.exp(col)), value * write], axis=1)
        solved = mm(inverse, right).astype(BF)
        wy_out[head, chunk * CHUNK : (chunk + 1) * CHUNK] = solved
        row = decay_rows[at : at + 1]
        end = row[:, CHUNK - 1 : CHUNK]
        maps.append((mm(flipped[chunk] * jnp.exp(end - row), solved), jnp.exp(end)))
    eye = jnp.where(row_ids == col_ids, 1.0, 0.0)
    for head in range(ratio):
        state = None
        for chunk in range(chunks):
            product, end = maps[head * chunks + chunk]
            linear = eye * end - product[:, :HD]
            added = product[:, HD:]
            if state is None:
                state = jnp.concatenate([linear, added], axis=1)
            else:
                starts_out[head, chunk - 1] = state.astype(BF)
                moved = mm(linear, state)
                state = jnp.concatenate([moved[:, :HD], moved[:, HD:] + added], axis=1)
        map_out[head] = state.astype(BF)


def output_kernel(
    ratio,
    chunks,
    query_ref,
    rims_ref,
    taps_ref,
    keys_ref,
    wy_ref,
    starts_ref,
    decay_ref,
    parts_out,
    stage,
):
    row_ids, col_ids = grid_ids()
    stage_rows(stage, rims_ref, query_ref)
    decay_rows, decay_cols = cumulated(decay_ref[0])
    taps = taps_ref[...]
    for chunk in range(chunks):
        rows = slice(chunk * CHUNK, (chunk + 1) * CHUNK)
        query = unit_rows(conv_chunk(stage, taps, chunk), HD ** (-0.5))
        scores = mm_nt(query, keys_ref[rows])
        for head in range(ratio):
            at = head * chunks + chunk
            col = decay_cols[:, at : at + 1]
            fading = jnp.exp(jnp.minimum(col - decay_rows[at : at + 1], 0.0))
            weights = jnp.where(row_ids >= col_ids, scores * fading, 0.0)
            scaled = query * jnp.exp(col)
            wy = wy_ref[head, rows]
            if chunk == 0:
                whole = mm(weights, wy)
                linear = scaled - whole[:, :HD]
                local = whole[:, HD:]
            else:
                state = starts_ref[head, chunk - 1]
                removed = mm(wy[:, :HD], state)
                left = jnp.concatenate([scaled, weights], axis=1)
                rest = jnp.concatenate(
                    [-removed[:, :HD], wy[:, HD:].astype(F32) - removed[:, HD:]], axis=1
                ).astype(BF)
                whole = mm(left, jnp.concatenate([state, rest], axis=0))
                linear = whole[:, :HD]
                local = whole[:, HD:]
            parts_out[head, rows, :HD] = linear.astype(BF)
            parts_out[head, rows, HD:] = local.astype(BF)


def final_kernel(heads, parts_ref, state_ref, gate_ref, weight_ref, out_ref, normed):
    for head in range(heads):
        lanes = slice(head * HD, (head + 1) * HD)
        attended = parts_ref[head, :, HD:].astype(F32) + mm(
            parts_ref[head, :, :HD], state_ref[head]
        )
        spread = lax.rsqrt(jnp.mean(attended * attended, axis=-1, keepdims=True) + 1e-06)
        normed[:, lanes] = (attended * spread * silu(gate_ref[:, lanes].astype(F32))).astype(BF)
    out_ref[...] = jnp.dot(normed[...], weight_ref[...], preferred_element_type=F32).astype(BF)


def exchanged(value, axis, bit):
    count = lax.axis_size(axis)
    return lax.ppermute(value, axis, [(source, source ^ bit) for source in range(count)])


def after(later, earlier):
    moved = jnp.einsum(
        "hij,hjf->hif", later[..., :HD].astype(BF), earlier.astype(BF), preferred_element_type=F32
    )
    return moved.at[..., HD:].add(later[..., HD:])


def incoming_state(total, axis):
    count = lax.axis_size(axis)
    index = lax.axis_index(axis)
    heads = total.shape[0]
    total = total.astype(F32)
    eye = jnp.broadcast_to(jnp.eye(HD, dtype=F32), (heads, HD, HD))
    before = jnp.concatenate([eye, jnp.zeros_like(eye)], axis=-1)
    bit = 1
    while bit < count:
        other = exchanged(total.astype(BF), axis, bit).astype(F32)
        high = (index & bit) != 0
        before = jnp.where(high, after(before, other), before)
        if 2 * bit < count:
            total = after(jnp.where(high, total, other), jnp.where(high, other, total))
        bit *= 2
    return before[..., HD:]


def scattered_sum(value, axis):
    count = lax.axis_size(axis)
    index = lax.axis_index(axis)
    parts = value.reshape(count, value.shape[0] // count, value.shape[1])

    def take(at):
        return lax.dynamic_index_in_dim(parts, jnp.clip(at, 0, count - 1), 0, keepdims=False)

    up = down = None
    for step in range(count - 1):
        send_up = take(count - 1 - step + index)
        send_down = take(step - (count - 1 - index))
        if up is not None:
            send_up = (send_up.astype(F32) + up.astype(F32)).astype(BF)
            send_down = (send_down.astype(F32) + down.astype(F32)).astype(BF)
        up = lax.ppermute(send_up, axis, [(z, z + 1) for z in range(step + 1)])
        down = lax.ppermute(
            send_down, axis, [(count - 1 - z, count - 2 - z) for z in range(step + 1)]
        )
    own = take(index).astype(F32)
    return (own + up.astype(F32) + down.astype(F32)).astype(BF)


def shards(
    inputs,
    w_query,
    w_key,
    w_value,
    w_gate_out,
    conv_query,
    conv_key,
    conv_value,
    decay_log,
    write_rate,
    w_out,
):
    def project(weights):
        return jnp.dot(inputs, weights, preferred_element_type=F32).astype(BF)

    proj_key = project(w_key)
    proj_value = project(w_value)
    proj_query = project(w_query)
    rows = inputs.shape[0]
    key_width = proj_key.shape[1]
    key_heads = key_width // HD
    heads = proj_value.shape[1] // HD
    ratio = heads // key_heads
    chunks = rows // CHUNK
    tails = jnp.concatenate(
        [proj_key[-RIM:], proj_value[-RIM:], proj_query[-RIM:]], axis=1
    )
    count = lax.axis_size("ctx")
    rims = lax.ppermute(tails, "ctx", [(at, at + 1) for at in range(count - 1)])
    gate_in = project(w_gate_out)
    rims_k = rims[:, :key_width]
    rims_v = rims[:, key_width : key_width + heads * HD]
    rims_q = rims[:, key_width + heads * HD :]
    decay = decay_log.reshape(key_heads, ratio * chunks, CHUNK)
    write = write_rate.reshape(key_heads, ratio * chunks, CHUNK)

    def cols(length, width):
        return pl.BlockSpec((length, width), lambda h: (0, h))

    gate_spec = pl.BlockSpec((1, ratio * chunks, CHUNK), lambda h: (h, 0, 0))
    wy_spec = pl.BlockSpec((ratio, rows, 2 * HD), lambda h: (h, 0, 0))
    starts_spec = pl.BlockSpec((ratio, chunks - 1, HD, 2 * HD), lambda h: (h, 0, 0, 0))
    taps_len = conv_key.shape[0]
    keys, wy, starts, total = pl.pallas_call(
        functools.partial(local_kernel, ratio, chunks),
        grid=(key_heads,),
        in_specs=[
            cols(rows, HD),
            cols(rows, ratio * HD),
            cols(RIM, HD),
            cols(RIM, ratio * HD),
            cols(taps_len, HD),
            cols(taps_len, ratio * HD),
            gate_spec,
            gate_spec,
        ],
        out_specs=[
            cols(rows, HD),
            wy_spec,
            starts_spec,
            pl.BlockSpec((ratio, HD, 2 * HD), lambda h: (h, 0, 0)),
        ],
        out_shape=[
            jax.ShapeDtypeStruct((rows, key_width), BF),
            jax.ShapeDtypeStruct((heads, rows, 2 * HD), BF),
            jax.ShapeDtypeStruct((heads, chunks - 1, HD, 2 * HD), BF),
            jax.ShapeDtypeStruct((heads, HD, 2 * HD), BF),
        ],
        scratch_shapes=[
            pltpu.VMEM((rows + 8, HD), F32),
            pltpu.VMEM((rows + 8, ratio * HD), F32),
        ],
        name="local",
    )(proj_key, proj_value, rims_k, rims_v, conv_key, conv_value, decay, write)
    parts = pl.pallas_call(
        functools.partial(output_kernel, ratio, chunks),
        grid=(key_heads,),
        in_specs=[
            cols(rows, HD),
            cols(RIM, HD),
            cols(taps_len, HD),
            cols(rows, HD),
            wy_spec,
            starts_spec,
            gate_spec,
        ],
        out_specs=wy_spec,
        out_shape=jax.ShapeDtypeStruct((heads, rows, 2 * HD), BF),
        scratch_shapes=[pltpu.VMEM((rows + 8, HD), F32)],
        name="outputs",
    )(proj_query, rims_q, conv_query, keys, wy, starts, decay)
    state = incoming_state(total, "ctx").astype(BF)
    width_out = w_out.shape[1]
    partial_out = pl.pallas_call(
        functools.partial(final_kernel, heads),
        grid=(chunks,),
        in_specs=[
            pl.BlockSpec((heads, CHUNK, 2 * HD), lambda c: (0, c, 0)),
            pl.BlockSpec((heads, HD, HD), lambda c: (0, 0, 0)),
            pl.BlockSpec((CHUNK, heads * HD), lambda c: (c, 0)),
            pl.BlockSpec((heads * HD, width_out), lambda c: (0, 0)),
        ],
        out_specs=pl.BlockSpec((CHUNK, width_out), lambda c: (c, 0)),
        out_shape=jax.ShapeDtypeStruct((rows, width_out), BF),
        scratch_shapes=[pltpu.VMEM((CHUNK, heads * HD), BF)],
        name="final",
    )(parts, state, gate_in, w_out)
    return scattered_sum(partial_out, "head")


def solution(mesh):
    return jax.shard_map(
        shards,
        mesh=mesh,
        in_specs=(
            P("ctx", None),
            P(None, "head"),
            P(None, "head"),
            P(None, "head"),
            P(None, "head"),
            P(None, "head"),
            P(None, "head"),
            P(None, "head"),
            P("head", "ctx"),
            P("head", "ctx"),
            P("head", None),
        ),
        out_specs=P(("ctx", "head"), None),
        check_vma=False,
    )
```

```python
import functools

import jax
import jax.numpy as jnp
from jax import lax
from jax.experimental import pallas as pl
from jax.experimental.pallas import tpu as pltpu
from jax.sharding import PartitionSpec as P

HD = 128
CHUNK = 128
RIM = 16
BF = jnp.bfloat16
F32 = jnp.float32
EXACT = lax.Precision.HIGHEST


def mm(left, right):
    return jnp.dot(left.astype(BF), right.astype(BF), preferred_element_type=F32)


def mm_nt(left, right):
    return lax.dot_general(
        left.astype(BF), right.astype(BF), (((1,), (1,)), ((), ())), preferred_element_type=F32
    )


def silu(values):
    return values / (1.0 + jnp.exp(-values))


def unit_rows(values, factor):
    return values * (lax.rsqrt(jnp.sum(values * values, axis=-1, keepdims=True) + 1e-06) * factor)


def stage_rows(stage, rims_ref, rows_ref):
    stage[0:8] = rims_ref[RIM - 8 : RIM].astype(F32)
    stage[8:] = rows_ref[...].astype(F32)


def conv_chunk(stage, taps, chunk):
    taps_len = taps.shape[0]
    start = 8 - (taps_len - 1) + chunk * CHUNK
    total = taps[0:1] * stage[start : start + CHUNK]
    for offset in range(1, taps_len):
        total = total + taps[offset : offset + 1] * stage[start + offset : start + offset + CHUNK]
    return silu(total)


def grid_ids():
    row_ids = lax.broadcasted_iota(jnp.int32, (CHUNK, CHUNK), 0)
    col_ids = lax.broadcasted_iota(jnp.int32, (CHUNK, CHUNK), 1)
    return row_ids, col_ids


def cumulated(decay):
    row_ids, col_ids = grid_ids()
    lower = jnp.where(row_ids >= col_ids, 1.0, 0.0)
    dims = (((1,), (1,)), ((), ()))
    as_rows = lax.dot_general(decay, lower, dims, precision=EXACT, preferred_element_type=F32)
    as_cols = lax.dot_general(lower, decay, dims, precision=EXACT, preferred_element_type=F32)
    return as_rows, as_cols


def head_rows(ref, ratio, chunks):
    start = pl.program_id(0) * ratio
    rows = [ref[pl.ds(start + head, 1), :] for head in range(ratio)]
    return jnp.concatenate(
        [
            row[:, chunk * CHUNK : (chunk + 1) * CHUNK]
            for chunk in range(chunks)
            for row in rows
        ],
        axis=0,
    )


def inverted(systems):
    row_ids, col_ids = grid_ids()
    same = row_ids // 2 == col_ids // 2
    eye = jnp.where(row_ids == col_ids, 1.0, 0.0)
    inverses = [eye - jnp.where(same, system, 0.0) for system in systems]
    size = 2
    while size < CHUNK:
        cross = (row_ids // (2 * size) == col_ids // (2 * size)) & (
            row_ids // size != col_ids // size
        )
        links = [jnp.where(cross, system, 0.0).astype(BF) for system in systems]
        halves = [inverse.astype(BF) for inverse in inverses]
        if size < 8:
            inner = [mm(link, half) for link, half in zip(links, halves)]
            outer = [mm(half, part) for half, part in zip(halves, inner)]
            inverses = [inverse - part for inverse, part in zip(inverses, outer)]
        else:
            starts = range(size, CHUNK, 2 * size)
            odd = [
                jnp.concatenate([inverse[s : s + size] for s in starts], axis=0)
                for inverse in inverses
            ]
            inner = [mm(part, link) for part, link in zip(odd, links)]
            outer = [mm(part, half) for part, half in zip(inner, halves)]
            odd = [part - update for part, update in zip(odd, outer)]
            inverses = [
                jnp.concatenate(
                    [
                        piece
                        for at, s in enumerate(starts)
                        for piece in (
                            inverse[s - size : s],
                            part[at * size : (at + 1) * size],
                        )
                    ],
                    axis=0,
                )
                for inverse, part in zip(inverses, odd)
            ]
        size *= 2
    return inverses


def local_kernel(
    ratio,
    chunks,
    keys_ref,
    values_ref,
    rims_k_ref,
    rims_v_ref,
    taps_k_ref,
    taps_v_ref,
    decay_ref,
    write_ref,
    keys_out,
    wy_out,
    starts_out,
    map_out,
    stage_k,
    stage_v,
):
    row_ids, col_ids = grid_ids()
    stage_rows(stage_k, rims_k_ref, keys_ref)
    stage_rows(stage_v, rims_v_ref, values_ref)
    decay_rows, decay_cols = cumulated(head_rows(decay_ref, ratio, chunks))
    write_cols = lax.dot_general(
        jnp.where(row_ids == col_ids, 1.0, 0.0),
        head_rows(write_ref, ratio, chunks),
        (((1,), (1,)), ((), ())),
        precision=EXACT,
        preferred_element_type=F32,
    )
    taps_k = taps_k_ref[...]
    taps_v = taps_v_ref[...]
    keys = []
    flipped = []
    values = []
    inner = []
    for chunk in range(chunks):
        key = unit_rows(conv_chunk(stage_k, taps_k, chunk), 1.0)
        keys_out[chunk * CHUNK : (chunk + 1) * CHUNK] = key.astype(BF)
        keys.append(key)
        flipped.append(key.T)
        inner.append(mm(key, flipped[-1]))
        values.append(conv_chunk(stage_v, taps_v, chunk))
    units = [(head, chunk) for head in range(ratio) for chunk in range(chunks)]
    systems = []
    for head, chunk in units:
        at = chunk * ratio + head
        fading = jnp.exp(
            jnp.minimum(decay_cols[:, at : at + 1] - decay_rows[at : at + 1], 0.0)
        )
        systems.append(
            jnp.where(
                row_ids > col_ids, write_cols[:, at : at + 1] * inner[chunk] * fading, 0.0
            )
        )
    inverses = inverted(systems)
    maps = []
    for (head, chunk), inverse in zip(units, inverses):
        at = chunk * ratio + head
        col = decay_cols[:, at : at + 1]
        write = write_cols[:, at : at + 1]
        value = values[chunk][:, head * HD : (head + 1) * HD]
        right = jnp.concatenate([keys[chunk] * (write * jnp.exp(col)), value * write], axis=1)
        solved = mm(inverse, right).astype(BF)
        wy_out[head, chunk * CHUNK : (chunk + 1) * CHUNK] = solved
        row = decay_rows[at : at + 1]
        end = row[:, CHUNK - 1 : CHUNK]
        maps.append((mm(flipped[chunk] * jnp.exp(end - row), solved), jnp.exp(end)))
    eye = jnp.where(row_ids == col_ids, 1.0, 0.0)
    for head in range(ratio):
        state = None
        for chunk in range(chunks):
            product, end = maps[head * chunks + chunk]
            linear = eye * end - product[:, :HD]
            added = product[:, HD:]
            if state is None:
                state = jnp.concatenate([linear, added], axis=1)
            else:
                starts_out[head, chunk - 1] = state.astype(BF)
                moved = mm(linear, state)
                state = jnp.concatenate([moved[:, :HD], moved[:, HD:] + added], axis=1)
        map_out[head] = state.astype(BF)


def output_kernel(
    ratio,
    chunks,
    query_ref,
    rims_ref,
    taps_ref,
    keys_ref,
    wy_ref,
    starts_ref,
    decay_ref,
    parts_out,
    stage,
):
    row_ids, col_ids = grid_ids()
    stage_rows(stage, rims_ref, query_ref)
    decay_rows, decay_cols = cumulated(head_rows(decay_ref, ratio, chunks))
    taps = taps_ref[...]
    for chunk in range(chunks):
        rows = slice(chunk * CHUNK, (chunk + 1) * CHUNK)
        query = unit_rows(conv_chunk(stage, taps, chunk), HD ** (-0.5))
        scores = mm_nt(query, keys_ref[rows])
        for head in range(ratio):
            at = chunk * ratio + head
            col = decay_cols[:, at : at + 1]
            fading = jnp.exp(jnp.minimum(col - decay_rows[at : at + 1], 0.0))
            weights = jnp.where(row_ids >= col_ids, scores * fading, 0.0)
            scaled = query * jnp.exp(col)
            wy = wy_ref[head, rows]
            if chunk == 0:
                whole = mm(weights, wy)
                linear = scaled - whole[:, :HD]
                local = whole[:, HD:]
            else:
                state = starts_ref[head, chunk - 1]
                removed = mm(wy[:, :HD], state)
                left = jnp.concatenate([scaled, weights], axis=1)
                rest = jnp.concatenate(
                    [-removed[:, :HD], wy[:, HD:].astype(F32) - removed[:, HD:]], axis=1
                ).astype(BF)
                whole = mm(left, jnp.concatenate([state, rest], axis=0))
                linear = whole[:, :HD]
                local = whole[:, HD:]
            parts_out[head, rows, :HD] = linear.astype(BF)
            parts_out[head, rows, HD:] = local.astype(BF)


def final_kernel(heads, first, plan_ref, parts_ref, kept_ref, got_ref, gate_ref, weight_ref, out_ref, normed):
    swap = plan_ref[0] != 0
    half = heads // 2
    for head in range(heads):
        lanes = slice(head * HD, (head + 1) * HD)
        kept, got = kept_ref[head % half], got_ref[head % half]
        state = jnp.where(swap, got, kept) if head < half else jnp.where(swap, kept, got)
        attended = parts_ref[head, :, HD:].astype(F32) + mm(parts_ref[head, :, :HD], state)
        spread = lax.rsqrt(jnp.mean(attended * attended, axis=-1, keepdims=True) + 1e-06)
        normed[:, lanes] = (attended * spread * silu(gate_ref[:, lanes].astype(F32))).astype(BF)
    out_ref[0] = jnp.dot(normed[...], weight_ref[...], preferred_element_type=F32).astype(BF)


def final_rows(first, count, plan, parts, kept, got, gate_in, w_out, length):
    heads = parts.shape[0]
    width = w_out.shape[1]
    return pl.pallas_call(
        functools.partial(final_kernel, heads, first),
        grid_spec=pltpu.PrefetchScalarGridSpec(
            num_scalar_prefetch=1,
            grid=(count,),
            in_specs=[
                pl.BlockSpec((heads, length, 2 * HD), lambda c, plan: (0, plan[1 + first + c], 0)),
                pl.BlockSpec(memory_space=pltpu.VMEM),
                pl.BlockSpec(memory_space=pltpu.VMEM),
                pl.BlockSpec((length, heads * HD), lambda c, plan: (plan[1 + first + c], 0)),
                pl.BlockSpec(memory_space=pltpu.VMEM),
            ],
            out_specs=pl.BlockSpec((1, length, width), lambda c, plan: (c, 0, 0)),
            scratch_shapes=[pltpu.VMEM((length, heads * HD), BF)],
        ),
        out_shape=jax.ShapeDtypeStruct((count, length, width), BF),
        compiler_params=pltpu.CompilerParams(vmem_limit_bytes=16 << 20),
        name="final",
    )(plan, parts, kept, got, gate_in, w_out)


def exchanged(value, axis, bit):
    count = lax.axis_size(axis)
    return lax.ppermute(value, axis, [(source, source ^ bit) for source in range(count)])


def after(later, earlier):
    moved = jnp.einsum(
        "hij,hjf->hif", later[..., :HD].astype(BF), earlier.astype(BF), preferred_element_type=F32
    )
    if earlier.shape[-1] == HD:
        return moved + later[..., HD:].astype(F32)
    return jnp.concatenate([moved[..., :HD], moved[..., HD:] + later[..., HD:].astype(F32)], axis=-1)


def incoming_state(total, axis, covers):
    covers = list(covers)
    count = lax.axis_size(axis)
    index = lax.axis_index(axis)

    def cover(value):
        for at, work in enumerate(covers):
            if work is not None:
                value, work = lax.optimization_barrier((value, work))
                done.append(work)
                covers[at] = None
                break
        return value

    done = []
    odd = (index & 1) != 0
    half = total.shape[0] // 2
    mine = jnp.where(odd, total[half:], total[:half])
    other = exchanged(jnp.where(odd, total[:half], total[half:]), axis, 1)
    first = jnp.where(odd, other, mine)
    second = jnp.where(odd, mine, other)
    total = after(second, first).astype(BF)
    before_map = before_state = None
    bit = 2
    while bit < count:
        high = (index & bit) != 0
        last = 2 * bit >= count
        if last and before_map is not None:
            pairs = [(at, at ^ bit) for at in range(count) if not at & bit]
            state = cover(lax.ppermute(total[..., HD:], axis, pairs))
            moved = after(jnp.concatenate([before_map, before_state], axis=-1), state)
            before_state = jnp.where(high, moved, before_state.astype(F32))
        else:
            other = cover(exchanged(total, axis, bit))
            if before_map is None:
                eye = jnp.broadcast_to(jnp.eye(HD, dtype=BF), (half, HD, HD))
                before_map = jnp.where(high, other[..., :HD], eye)
                before_state = jnp.where(high, other[..., HD:], jnp.zeros((), BF))
            else:
                before = jnp.concatenate([before_map, before_state], axis=-1)
                moved = jnp.where(high, after(before, other), before.astype(F32)).astype(BF)
                before_map, before_state = moved[..., :HD], moved[..., HD:]
            if not last:
                total = after(
                    jnp.where(high, total, other), jnp.where(high, other, total)
                ).astype(BF)
        bit *= 2
    if before_state is None:
        before_state = jnp.zeros((half, HD, HD), F32)
    before_state = before_state.astype(BF)
    passed = after(first, before_state).astype(BF)
    kept = jnp.where(odd, passed, before_state)
    got = exchanged(jnp.where(odd, before_state, passed), axis, 1)
    done.extend(work for work in covers if work is not None)
    return kept, got, done


def summed(*values):
    total = values[0].astype(F32)
    for value in values[1:]:
        total = total + value.astype(F32)
    return total.astype(BF)


def line_sum(parts, axis):
    count = lax.axis_size(axis)
    index = lax.axis_index(axis)

    def take(at):
        return lax.dynamic_index_in_dim(parts, jnp.clip(at, 0, count - 1), 0, keepdims=False)

    up = down = None
    for step in range(count - 1):
        send_up = take(count - 1 - step + index)
        send_down = take(step - (count - 1 - index))
        if up is not None:
            send_up = summed(send_up, up)
            send_down = summed(send_down, down)
        up = lax.ppermute(send_up, axis, [(z, z + 1) for z in range(step + 1)])
        down = lax.ppermute(
            send_down, axis, [(count - 1 - z, count - 2 - z) for z in range(step + 1)]
        )
    return summed(take(index), up, down)


def swapped_sum(far, rest, axis):
    pass_far, pass_near, own = rest
    width = far.shape[-1] // 2
    across = []
    for piece in (slice(0, width), slice(width, 2 * width)):
        paired = summed(pass_far[:, piece], exchanged(far[:, piece], axis, 1))
        across.append(exchanged(paired, axis, 2))
    near = exchanged(pass_near, axis, 1)
    return jnp.concatenate(
        [
            summed(own[:, at * width : (at + 1) * width], near[:, at * width : (at + 1) * width], part)
            for at, part in enumerate(across)
        ],
        axis=-1,
    )


def shards(
    inputs,
    w_query,
    w_key,
    w_value,
    w_gate_out,
    conv_query,
    conv_key,
    conv_value,
    decay_log,
    write_rate,
    w_out,
):
    def project(weights):
        return jnp.dot(inputs, weights, preferred_element_type=F32).astype(BF)

    proj_key = project(w_key)
    proj_value = project(w_value)
    proj_query = project(w_query)
    rows = inputs.shape[0]
    key_width = proj_key.shape[1]
    key_heads = key_width // HD
    heads = proj_value.shape[1] // HD
    ratio = heads // key_heads
    chunks = rows // CHUNK
    tails = jnp.concatenate(
        [proj_key[-RIM:], proj_value[-RIM:], proj_query[-RIM:]], axis=1
    )
    count = lax.axis_size("ctx")
    rims = lax.ppermute(tails, "ctx", [(at, at + 1) for at in range(count - 1)])
    gate_in = project(w_gate_out)
    def cols(length, width, start=0):
        return pl.BlockSpec((length, width), lambda h: (0, h + start // width))

    gate_spec = pl.BlockSpec((heads, rows), lambda h: (0, 0))
    wy_spec = pl.BlockSpec((ratio, rows, 2 * HD), lambda h: (h, 0, 0))
    starts_spec = pl.BlockSpec((ratio, chunks - 1, HD, 2 * HD), lambda h: (h, 0, 0, 0))
    taps_len = conv_key.shape[0]
    keys, wy, starts, total = pl.pallas_call(
        functools.partial(local_kernel, ratio, chunks),
        grid=(key_heads,),
        in_specs=[
            cols(rows, HD),
            cols(rows, ratio * HD),
            cols(RIM, HD),
            cols(RIM, ratio * HD, key_width),
            cols(taps_len, HD),
            cols(taps_len, ratio * HD),
            gate_spec,
            gate_spec,
        ],
        out_specs=[
            cols(rows, HD),
            wy_spec,
            starts_spec,
            pl.BlockSpec((ratio, HD, 2 * HD), lambda h: (h, 0, 0)),
        ],
        out_shape=[
            jax.ShapeDtypeStruct((rows, key_width), BF),
            jax.ShapeDtypeStruct((heads, rows, 2 * HD), BF),
            jax.ShapeDtypeStruct((heads, chunks - 1, HD, 2 * HD), BF),
            jax.ShapeDtypeStruct((heads, HD, 2 * HD), BF),
        ],
        scratch_shapes=[
            pltpu.VMEM((rows + 8, HD), F32),
            pltpu.VMEM((rows + 8, ratio * HD), F32),
        ],
        compiler_params=pltpu.CompilerParams(vmem_limit_bytes=24 << 20),
        name="local",
    )(proj_key, proj_value, rims, rims, conv_key, conv_value, decay_log, write_rate)
    parts = pl.pallas_call(
        functools.partial(output_kernel, ratio, chunks),
        grid=(key_heads,),
        in_specs=[
            cols(rows, HD),
            cols(RIM, HD, key_width + heads * HD),
            cols(taps_len, HD),
            cols(rows, HD),
            wy_spec,
            starts_spec,
            gate_spec,
        ],
        out_specs=wy_spec,
        out_shape=jax.ShapeDtypeStruct((heads, rows, 2 * HD), BF),
        scratch_shapes=[pltpu.VMEM((rows + 8, HD), F32)],
        compiler_params=pltpu.CompilerParams(vmem_limit_bytes=20 << 20),
        name="outputs",
    )(proj_query, rims, conv_query, keys, wy, starts, decay_log)
    kept, got, (parts, gate_in) = incoming_state(total, "ctx", (parts, gate_in))
    spread = lax.axis_size("head")
    place = lax.axis_index("head")
    length = rows // spread
    swap = lax.axis_index("ctx") & 1
    if spread == 4:
        order = [place ^ 3, place ^ 2, place ^ 1, place]
    else:
        order = list(range(spread))
    plan = jnp.stack([jnp.int32(at) for at in [swap] + order])
    shared = (plan, parts, kept, got, gate_in, w_out, length)
    if spread == 4:
        far = final_rows(0, 1, *shared)
        rest = final_rows(1, 3, *shared)
        return swapped_sum(far[0], rest, "head")
    return line_sum(final_rows(0, spread, *shared), "head")


def solution(mesh):
    return jax.shard_map(
        shards,
        mesh=mesh,
        in_specs=(
            P("ctx", None),
            P(None, "head"),
            P(None, "head"),
            P(None, "head"),
            P(None, "head"),
            P(None, "head"),
            P(None, "head"),
            P(None, "head"),
            P("head", "ctx"),
            P("head", "ctx"),
            P("head", None),
        ),
        out_specs=P(("ctx", "head"), None),
        check_vma=False,
    )
```

```python
import functools

import jax
import jax.numpy as jnp
from jax import lax
from jax.experimental import pallas as pl
from jax.experimental.pallas import tpu as pltpu
from jax.sharding import PartitionSpec as P

HD = 128
CHUNK = 128
RIM = 16
BF = jnp.bfloat16
F32 = jnp.float32
EXACT = lax.Precision.HIGHEST
WHOLE = pl.BlockSpec(memory_space=pltpu.VMEM)


def cost(matmul_rows, exps, size):
    return pl.CostEstimate(
        flops=2 * HD * HD * matmul_rows, transcendentals=exps, bytes_accessed=size
    )


def in_hbm(array):
    return pltpu.with_memory_space_constraint(array, pltpu.HBM)


def mm(left, right):
    return jnp.dot(left.astype(BF), right.astype(BF), preferred_element_type=F32)


def mm_nt(left, right):
    return lax.dot_general(
        left.astype(BF), right.astype(BF), (((1,), (1,)), ((), ())), preferred_element_type=F32
    )


def silu(values):
    return values / (1.0 + jnp.exp(-values))


def unit_rows(values, factor):
    return values * (lax.rsqrt(jnp.sum(values * values, axis=-1, keepdims=True) + 1e-06) * factor)


def stage_rows(stage, rims_ref, rows_ref):
    stage[0:8] = rims_ref[RIM - 8 : RIM].astype(F32)
    stage[8:] = rows_ref[...].astype(F32)


def conv_chunk(stage, taps, chunk):
    taps_len = taps.shape[0]
    start = 8 - (taps_len - 1) + chunk * CHUNK
    total = taps[0:1] * stage[start : start + CHUNK]
    for offset in range(1, taps_len):
        total = total + taps[offset : offset + 1] * stage[start + offset : start + offset + CHUNK]
    return silu(total)


def grid_ids():
    row_ids = lax.broadcasted_iota(jnp.int32, (CHUNK, CHUNK), 0)
    col_ids = lax.broadcasted_iota(jnp.int32, (CHUNK, CHUNK), 1)
    return row_ids, col_ids


def cumulated(decay):
    row_ids, col_ids = grid_ids()
    lower = jnp.where(row_ids >= col_ids, 1.0, 0.0)
    dims = (((1,), (1,)), ((), ()))
    as_rows = lax.dot_general(decay, lower, dims, precision=EXACT, preferred_element_type=F32)
    as_cols = lax.dot_general(lower, decay, dims, precision=EXACT, preferred_element_type=F32)
    return as_rows, as_cols


def head_rows(ref, ratio, chunks, group=1, member=0):
    start = (pl.program_id(0) * group + member) * ratio
    rows = [ref[pl.ds(start + head, 1), :] for head in range(ratio)]
    return jnp.concatenate(
        [
            row[:, chunk * CHUNK : (chunk + 1) * CHUNK]
            for chunk in range(chunks)
            for row in rows
        ],
        axis=0,
    )


def inverted(systems):
    row_ids, col_ids = grid_ids()
    same = row_ids // 2 == col_ids // 2
    eye = jnp.where(row_ids == col_ids, 1.0, 0.0)
    inverses = [eye - jnp.where(same, system, 0.0) for system in systems]
    size = 2
    while size < CHUNK:
        cross = (row_ids // (2 * size) == col_ids // (2 * size)) & (
            row_ids // size != col_ids // size
        )
        links = [jnp.where(cross, system, 0.0).astype(BF) for system in systems]
        halves = [inverse.astype(BF) for inverse in inverses]
        if size < 8:
            inner = [mm(link, half) for link, half in zip(links, halves)]
            outer = [mm(half, part) for half, part in zip(halves, inner)]
            inverses = [inverse - part for inverse, part in zip(inverses, outer)]
        else:
            starts = range(size, CHUNK, 2 * size)
            odd = [
                jnp.concatenate([inverse[s : s + size] for s in starts], axis=0)
                for inverse in inverses
            ]
            inner = [mm(part, link) for part, link in zip(odd, links)]
            outer = [mm(part, half) for part, half in zip(inner, halves)]
            odd = [part - update for part, update in zip(odd, outer)]
            inverses = [
                jnp.concatenate(
                    [
                        piece
                        for at, s in enumerate(starts)
                        for piece in (
                            inverse[s - size : s],
                            part[at * size : (at + 1) * size],
                        )
                    ],
                    axis=0,
                )
                for inverse, part in zip(inverses, odd)
            ]
        size *= 2
    return inverses


def local_kernel(
    group,
    ratio,
    chunks,
    keys_ref,
    values_ref,
    rims_k_ref,
    rims_v_ref,
    taps_k_ref,
    taps_v_ref,
    decay_ref,
    write_ref,
    keys_out,
    wy_out,
    starts_out,
    map_out,
    stage_k,
    stage_v,
):
    row_ids, col_ids = grid_ids()
    eye = jnp.where(row_ids == col_ids, 1.0, 0.0)
    stage_rows(stage_k, rims_k_ref, keys_ref)
    stage_rows(stage_v, rims_v_ref, values_ref)
    taps_k = taps_k_ref[...]
    taps_v = taps_v_ref[...]
    decays = []
    writes = []
    for member in range(group):
        decays.append(cumulated(head_rows(decay_ref, ratio, chunks, group, member)))
        writes.append(
            lax.dot_general(
                eye,
                head_rows(write_ref, ratio, chunks, group, member),
                (((1,), (1,)), ((), ())),
                precision=EXACT,
                preferred_element_type=F32,
            )
        )
    keys = {}
    flipped = {}
    values = []
    inner = {}
    for chunk in range(chunks):
        rows = slice(chunk * CHUNK, (chunk + 1) * CHUNK)
        smoothed = conv_chunk(stage_k, taps_k, chunk)
        values.append(conv_chunk(stage_v, taps_v, chunk))
        for member in range(group):
            lanes = slice(member * HD, (member + 1) * HD)
            key = unit_rows(smoothed[:, lanes], 1.0)
            keys_out[rows, lanes] = key.astype(BF)
            keys[member, chunk] = key
            flipped[member, chunk] = key.T
            inner[member, chunk] = mm(key, flipped[member, chunk])
    units = [
        (member, head, chunk)
        for member in range(group)
        for head in range(ratio)
        for chunk in range(chunks)
    ]
    systems = []
    for member, head, chunk in units:
        at = chunk * ratio + head
        decay_rows, decay_cols = decays[member]
        fading = jnp.exp(
            jnp.minimum(decay_cols[:, at : at + 1] - decay_rows[at : at + 1], 0.0)
        )
        systems.append(
            jnp.where(
                row_ids > col_ids,
                writes[member][:, at : at + 1] * inner[member, chunk] * fading,
                0.0,
            )
        )
    inverses = inverted(systems)
    maps = {}
    for (member, head, chunk), inverse in zip(units, inverses):
        at = chunk * ratio + head
        place = member * ratio + head
        decay_rows, decay_cols = decays[member]
        col = decay_cols[:, at : at + 1]
        write = writes[member][:, at : at + 1]
        value = values[chunk][:, place * HD : (place + 1) * HD]
        right = jnp.concatenate(
            [keys[member, chunk] * (write * jnp.exp(col)), value * write], axis=1
        )
        solved = mm(inverse, right).astype(BF)
        wy_out[place, chunk * CHUNK : (chunk + 1) * CHUNK] = solved
        row = decay_rows[at : at + 1]
        end = row[:, CHUNK - 1 : CHUNK]
        maps[place, chunk] = (
            mm(flipped[member, chunk] * jnp.exp(end - row), solved),
            jnp.exp(end),
        )
    states = [None] * (group * ratio)
    for chunk in range(chunks):
        for place, state in enumerate(states):
            product, end = maps[place, chunk]
            linear = eye * end - product[:, :HD]
            added = product[:, HD:]
            if state is None:
                states[place] = jnp.concatenate([linear, added], axis=1)
            else:
                starts_out[place, chunk - 1] = state.astype(BF)
                moved = mm(linear, state)
                states[place] = jnp.concatenate([moved[:, :HD], moved[:, HD:] + added], axis=1)
    for place, state in enumerate(states):
        map_out[place] = state.astype(BF)


def output_kernel(
    group,
    ratio,
    chunks,
    query_ref,
    rims_ref,
    taps_ref,
    keys_ref,
    wy_ref,
    starts_ref,
    decay_ref,
    parts_out,
    stage,
):
    row_ids, col_ids = grid_ids()
    stage_rows(stage, rims_ref, query_ref)
    decays = [
        cumulated(head_rows(decay_ref, ratio, chunks, group, member)) for member in range(group)
    ]
    taps = taps_ref[...]
    for chunk in range(chunks):
        rows = slice(chunk * CHUNK, (chunk + 1) * CHUNK)
        smoothed = conv_chunk(stage, taps, chunk)
        places = range(group * ratio)
        queries, scores = [], []
        for member in range(group):
            lanes = slice(member * HD, (member + 1) * HD)
            queries.append(unit_rows(smoothed[:, lanes], HD ** (-0.5)))
            scores.append(mm_nt(queries[-1], keys_ref[rows, lanes]))
        if chunk > 0:
            removed = [
                mm(wy_ref[place, rows, :HD], starts_ref[place, chunk - 1]) for place in places
            ]
        for place in places:
            member, head = divmod(place, ratio)
            at = chunk * ratio + head
            decay_rows, decay_cols = decays[member]
            col = decay_cols[:, at : at + 1]
            fading = jnp.exp(jnp.minimum(col - decay_rows[at : at + 1], 0.0))
            weights = jnp.where(row_ids >= col_ids, scores[member] * fading, 0.0)
            scaled = queries[member] * jnp.exp(col)
            wy = wy_ref[place, rows]
            if chunk == 0:
                whole = mm(weights, wy)
                linear = scaled - whole[:, :HD]
                local = whole[:, HD:]
            else:
                gone = removed[place]
                left = jnp.concatenate([scaled, weights], axis=1)
                rest = jnp.concatenate(
                    [-gone[:, :HD], wy[:, HD:].astype(F32) - gone[:, HD:]], axis=1
                ).astype(BF)
                whole = mm(
                    left, jnp.concatenate([starts_ref[place, chunk - 1], rest], axis=0)
                )
                linear = whole[:, :HD]
                local = whole[:, HD:]
            parts_out[place, rows, :HD] = linear.astype(BF)
            parts_out[place, rows, HD:] = local.astype(BF)


def norm_kernel(heads, swap_ref, parts_ref, kept_ref, got_ref, gate_ref, normed_ref):
    swap = swap_ref[0] != 0
    half = heads // 2
    for head in range(heads):
        lanes = slice(head * HD, (head + 1) * HD)
        kept, got = kept_ref[head % half], got_ref[head % half]
        state = jnp.where(swap, got, kept) if head < half else jnp.where(swap, kept, got)
        attended = parts_ref[head, :, HD:].astype(F32) + mm(parts_ref[head, :, :HD], state)
        spread = lax.rsqrt(jnp.mean(attended * attended, axis=-1, keepdims=True) + 1e-06)
        normed_ref[:, lanes] = (
            attended * spread * silu(gate_ref[:, lanes].astype(F32))
        ).astype(BF)


def final_rows(first, count, plan, parts, kept, got, gate_in, w_out, length):
    heads = parts.shape[0]
    normed = pl.pallas_call(
        functools.partial(norm_kernel, heads),
        grid_spec=pltpu.PrefetchScalarGridSpec(
            num_scalar_prefetch=1,
            grid=(count,),
            in_specs=[
                pl.BlockSpec((heads, length, 2 * HD), lambda c, plan: (0, plan[1 + first + c], 0)),
                WHOLE,
                WHOLE,
                pl.BlockSpec((length, heads * HD), lambda c, plan: (plan[1 + first + c], 0)),
            ],
            out_specs=pl.BlockSpec((length, heads * HD), lambda c, plan: (c, 0)),
        ),
        out_shape=jax.ShapeDtypeStruct((count * length, heads * HD), BF),
        compiler_params=pltpu.CompilerParams(vmem_limit_bytes=16 << 20),
        cost_estimate=cost(
            heads * count * length, heads * count * length * HD, 8 * heads * count * length * HD
        ),
        name="normed",
    )(plan, in_hbm(parts), kept, got, gate_in)
    mixed = jnp.dot(normed, w_out, preferred_element_type=F32).astype(BF)
    return mixed.reshape(count, length, w_out.shape[1])


def exchanged(value, axis, bit):
    count = lax.axis_size(axis)
    return lax.ppermute(value, axis, [(source, source ^ bit) for source in range(count)])


def after(later, earlier):
    moved = jnp.einsum(
        "hij,hjf->hif", later[..., :HD].astype(BF), earlier.astype(BF), preferred_element_type=F32
    )
    if earlier.shape[-1] == HD:
        return moved + later[..., HD:].astype(F32)
    return jnp.concatenate([moved[..., :HD], moved[..., HD:] + later[..., HD:].astype(F32)], axis=-1)


def incoming_state(total, axis, covers):
    covers = list(covers)
    count = lax.axis_size(axis)
    index = lax.axis_index(axis)

    def cover(value):
        for at, work in enumerate(covers):
            if work is not None:
                value, work = lax.optimization_barrier((value, work))
                done.append(work)
                covers[at] = None
                break
        return value

    done = []
    odd = (index & 1) != 0
    half = total.shape[0] // 2
    mine = jnp.where(odd, total[half:], total[:half])
    other = exchanged(jnp.where(odd, total[:half], total[half:]), axis, 1)
    first = jnp.where(odd, other, mine)
    second = jnp.where(odd, mine, other)
    total = after(second, first).astype(BF)
    before_map = before_state = None
    bit = 2
    while bit < count:
        high = (index & bit) != 0
        last = 2 * bit >= count
        if last and before_map is not None:
            pairs = [(at, at ^ bit) for at in range(count) if not at & bit]
            state = cover(lax.ppermute(total[..., HD:], axis, pairs))
            moved = after(jnp.concatenate([before_map, before_state], axis=-1), state)
            before_state = jnp.where(high, moved, before_state.astype(F32))
        else:
            other = cover(exchanged(total, axis, bit))
            if before_map is None:
                eye = jnp.broadcast_to(jnp.eye(HD, dtype=BF), (half, HD, HD))
                before_map = jnp.where(high, other[..., :HD], eye)
                before_state = jnp.where(high, other[..., HD:], jnp.zeros((), BF))
            else:
                before = jnp.concatenate([before_map, before_state], axis=-1)
                moved = jnp.where(high, after(before, other), before.astype(F32)).astype(BF)
                before_map, before_state = moved[..., :HD], moved[..., HD:]
            if not last:
                total = after(
                    jnp.where(high, total, other), jnp.where(high, other, total)
                ).astype(BF)
        bit *= 2
    if before_state is None:
        before_state = jnp.zeros((half, HD, HD), F32)
    before_state = before_state.astype(BF)
    passed = after(first, before_state).astype(BF)
    kept = jnp.where(odd, passed, before_state)
    got = exchanged(jnp.where(odd, before_state, passed), axis, 1)
    done.extend(work for work in covers if work is not None)
    return kept, got, done


def summed(*values):
    total = values[0].astype(F32)
    for value in values[1:]:
        total = total + value.astype(F32)
    return total.astype(BF)


def line_sum(parts, axis):
    count = lax.axis_size(axis)
    index = lax.axis_index(axis)

    def take(at):
        return lax.dynamic_index_in_dim(parts, jnp.clip(at, 0, count - 1), 0, keepdims=False)

    up = down = None
    for step in range(count - 1):
        send_up = take(count - 1 - step + index)
        send_down = take(step - (count - 1 - index))
        if up is not None:
            send_up = summed(send_up, up)
            send_down = summed(send_down, down)
        up = lax.ppermute(send_up, axis, [(z, z + 1) for z in range(step + 1)])
        down = lax.ppermute(
            send_down, axis, [(count - 1 - z, count - 2 - z) for z in range(step + 1)]
        )
    return summed(take(index), up, down)


def swapped_sum(rows_of, axis):
    far = rows_of(0, 1, None)[0]
    width = far.shape[-1] // 4
    early, late = slice(0, width), slice(width, 4 * width)
    first_in = exchanged(far[:, early], axis, 1)
    passed = rows_of(1, 1, None)[0]
    far_late, passed = lax.optimization_barrier((far[:, late], passed))
    later_in = exchanged(far_late, axis, 1)
    paired = summed(passed[:, early], first_in)
    first = exchanged(paired, axis, 2)
    rest = rows_of(2, 2, paired)
    later_in, first = lax.optimization_barrier((later_in, first))
    later = exchanged(summed(passed[:, late], later_in), axis, 2)
    near = exchanged(rest[0], axis, 1)
    own = rest[1]
    return jnp.concatenate(
        [
            summed(own[:, early], near[:, early], first),
            summed(own[:, late], near[:, late], later),
        ],
        axis=-1,
    )


def shards(
    inputs,
    w_query,
    w_key,
    w_value,
    w_gate_out,
    conv_query,
    conv_key,
    conv_value,
    decay_log,
    write_rate,
    w_out,
):
    def project(weights):
        return jnp.dot(inputs, weights, preferred_element_type=F32).astype(BF)

    proj_key = project(w_key)
    proj_value = project(w_value)
    proj_query = project(w_query)
    rows = inputs.shape[0]
    key_width = proj_key.shape[1]
    key_heads = key_width // HD
    heads = proj_value.shape[1] // HD
    ratio = heads // key_heads
    chunks = rows // CHUNK
    tails = jnp.concatenate(
        [proj_key[-RIM:], proj_value[-RIM:], proj_query[-RIM:]], axis=1
    )
    count = lax.axis_size("ctx")
    rims = lax.ppermute(tails, "ctx", [(at, at + 1) for at in range(count - 1)])
    gate_in = project(w_gate_out)
    group = 2 if key_heads % 2 == 0 else 1

    def cols(length, width, start=0):
        return pl.BlockSpec((length, group * width), lambda h: (0, h + start // (group * width)))

    gate_spec = pl.BlockSpec((heads, rows), lambda h: (0, 0))
    wy_spec = pl.BlockSpec((group * ratio, rows, 2 * HD), lambda h: (h, 0, 0))
    starts_spec = pl.BlockSpec((group * ratio, chunks - 1, HD, 2 * HD), lambda h: (h, 0, 0, 0))
    taps_len = conv_key.shape[0]
    keys, wy, starts, total = pl.pallas_call(
        functools.partial(local_kernel, group, ratio, chunks),
        grid=(key_heads // group,),
        in_specs=[
            cols(rows, HD),
            cols(rows, ratio * HD),
            cols(RIM, HD),
            cols(RIM, ratio * HD, key_width),
            cols(taps_len, HD),
            cols(taps_len, ratio * HD),
            gate_spec,
            gate_spec,
        ],
        out_specs=[
            cols(rows, HD),
            wy_spec,
            starts_spec,
            pl.BlockSpec((group * ratio, HD, 2 * HD), lambda h: (h, 0, 0)),
        ],
        out_shape=[
            pltpu.HBM((rows, key_width), BF),
            pltpu.HBM((heads, rows, 2 * HD), BF),
            pltpu.HBM((heads, chunks - 1, HD, 2 * HD), BF),
            jax.ShapeDtypeStruct((heads, HD, 2 * HD), BF),
        ],
        scratch_shapes=[
            pltpu.VMEM((rows + 8, group * HD), F32),
            pltpu.VMEM((rows + 8, group * ratio * HD), F32),
        ],
        compiler_params=pltpu.CompilerParams(vmem_limit_bytes=32 << 20),
        cost_estimate=cost(16 * heads * rows, 4 * heads * rows * HD, 12 * heads * rows * HD),
        name="local",
    )(in_hbm(proj_key), in_hbm(proj_value), rims, rims, conv_key, conv_value, decay_log, write_rate)
    parts = pl.pallas_call(
        functools.partial(output_kernel, group, ratio, chunks),
        grid=(key_heads // group,),
        in_specs=[
            cols(rows, HD),
            cols(RIM, HD, key_width + heads * HD),
            cols(taps_len, HD),
            cols(rows, HD),
            wy_spec,
            starts_spec,
            gate_spec,
        ],
        out_specs=wy_spec,
        out_shape=pltpu.HBM((heads, rows, 2 * HD), BF),
        scratch_shapes=[pltpu.VMEM((rows + 8, group * HD), F32)],
        compiler_params=pltpu.CompilerParams(vmem_limit_bytes=24 << 20),
        cost_estimate=cost(8 * heads * rows, 2 * heads * rows * HD, 12 * heads * rows * HD),
        name="outputs",
    )(in_hbm(proj_query), rims, conv_query, in_hbm(keys), in_hbm(wy), in_hbm(starts), decay_log)
    kept, got, (parts, gate_in) = incoming_state(total, "ctx", (parts, gate_in))
    spread = lax.axis_size("head")
    place = lax.axis_index("head")
    length = rows // spread
    swap = lax.axis_index("ctx") & 1
    if spread == 4:
        order = [place ^ 3, place ^ 2, place ^ 1, place]
    else:
        order = list(range(spread))
    plan = jnp.stack([jnp.int32(at) for at in [swap] + order])

    def rows_of(first, amount, earlier):
        steps = plan
        if earlier is not None:
            steps, _ = lax.optimization_barrier((plan, earlier))
        return final_rows(first, amount, steps, parts, kept, got, gate_in, w_out, length)

    if spread == 4:
        return swapped_sum(rows_of, "head")
    return line_sum(rows_of(0, spread, None), "head")


def solution(mesh):
    return jax.shard_map(
        shards,
        mesh=mesh,
        in_specs=(
            P("ctx", None),
            P(None, "head"),
            P(None, "head"),
            P(None, "head"),
            P(None, "head"),
            P(None, "head"),
            P(None, "head"),
            P(None, "head"),
            P("head", "ctx"),
            P("head", "ctx"),
            P("head", None),
        ),
        out_specs=P(("ctx", "head"), None),
        check_vma=False,
    )
```

```python
import functools

import jax
import jax.numpy as jnp
from jax import lax
from jax.experimental import pallas as pl
from jax.experimental.pallas import tpu as pltpu
from jax.sharding import PartitionSpec as P

HD = 128
CHUNK = 128
RIM = 8
BF = jnp.bfloat16
F32 = jnp.float32
EXACT = lax.Precision.HIGHEST
SCALAR = pl.BlockSpec(memory_space=pltpu.SMEM)
WHOLE = pl.BlockSpec(memory_space=pltpu.VMEM)


def cost(matmul_rows, exps, size):
    return pl.CostEstimate(
        flops=2 * HD * HD * matmul_rows, transcendentals=exps, bytes_accessed=size
    )


def in_hbm(array):
    return pltpu.with_memory_space_constraint(array, pltpu.HBM)


def mm(left, right):
    return jnp.dot(left.astype(BF), right.astype(BF), preferred_element_type=F32)


def mm_nt(left, right):
    return lax.dot_general(
        left.astype(BF), right.astype(BF), (((1,), (1,)), ((), ())), preferred_element_type=F32
    )


def silu(values):
    return values / (1.0 + jnp.exp(-values))


def unit_rows(values, factor):
    return values * (lax.rsqrt(jnp.sum(values * values, axis=-1, keepdims=True) + 1e-06) * factor)


def stage_rows(stage, at_ref, rims_ref, rows_ref):
    stage[0:8] = jnp.where(at_ref[0] > 0, rims_ref[RIM - 8 : RIM].astype(F32), 0.0)
    stage[8:] = rows_ref[...].astype(F32)


def conv_chunk(stage, taps, chunk):
    taps_len = taps.shape[0]
    start = 8 - (taps_len - 1) + chunk * CHUNK
    total = taps[0:1] * stage[start : start + CHUNK]
    for offset in range(1, taps_len):
        total = total + taps[offset : offset + 1] * stage[start + offset : start + offset + CHUNK]
    return silu(total)


def grid_ids():
    row_ids = lax.broadcasted_iota(jnp.int32, (CHUNK, CHUNK), 0)
    col_ids = lax.broadcasted_iota(jnp.int32, (CHUNK, CHUNK), 1)
    return row_ids, col_ids


def cumulated(decay):
    row_ids, col_ids = grid_ids()
    lower = jnp.where(row_ids >= col_ids, 1.0, 0.0)
    dims = (((1,), (1,)), ((), ()))
    as_rows = lax.dot_general(decay, lower, dims, precision=EXACT, preferred_element_type=F32)
    as_cols = lax.dot_general(lower, decay, dims, precision=EXACT, preferred_element_type=F32)
    return as_rows, as_cols


def head_rows(ref, ratio, chunks, group=1, member=0):
    start = (pl.program_id(0) * group + member) * ratio
    rows = [ref[pl.ds(start + head, 1), :] for head in range(ratio)]
    return jnp.concatenate(
        [
            row[:, chunk * CHUNK : (chunk + 1) * CHUNK]
            for chunk in range(chunks)
            for row in rows
        ],
        axis=0,
    )


def inverted(systems):
    row_ids, col_ids = grid_ids()
    same = row_ids // 2 == col_ids // 2
    eye = jnp.where(row_ids == col_ids, 1.0, 0.0)
    inverses = [eye - jnp.where(same, system, 0.0) for system in systems]
    size = 2
    while size < CHUNK:
        cross = (row_ids // (2 * size) == col_ids // (2 * size)) & (
            row_ids // size != col_ids // size
        )
        links = [jnp.where(cross, system, 0.0).astype(BF) for system in systems]
        halves = [inverse.astype(BF) for inverse in inverses]
        if size < 8:
            inner = [mm(link, half) for link, half in zip(links, halves)]
            outer = [mm(half, part) for half, part in zip(halves, inner)]
            inverses = [inverse - part for inverse, part in zip(inverses, outer)]
        else:
            starts = range(size, CHUNK, 2 * size)
            odd = [
                jnp.concatenate([inverse[s : s + size] for s in starts], axis=0)
                for inverse in inverses
            ]
            inner = [mm(part, link) for part, link in zip(odd, links)]
            outer = [mm(part, half) for part, half in zip(inner, halves)]
            odd = [part - update for part, update in zip(odd, outer)]
            inverses = [
                jnp.concatenate(
                    [
                        piece
                        for at, s in enumerate(starts)
                        for piece in (
                            inverse[s - size : s],
                            part[at * size : (at + 1) * size],
                        )
                    ],
                    axis=0,
                )
                for inverse, part in zip(inverses, odd)
            ]
        size *= 2
    return inverses


def local_kernel(
    group,
    ratio,
    chunks,
    at_ref,
    keys_ref,
    values_ref,
    rims_k_ref,
    rims_v_ref,
    taps_k_ref,
    taps_v_ref,
    decay_ref,
    write_ref,
    keys_out,
    wy_out,
    starts_out,
    map_out,
    stage_k,
    stage_v,
):
    row_ids, col_ids = grid_ids()
    eye = jnp.where(row_ids == col_ids, 1.0, 0.0)
    stage_rows(stage_k, at_ref, rims_k_ref, keys_ref)
    stage_rows(stage_v, at_ref, rims_v_ref, values_ref)
    taps_k = taps_k_ref[...]
    taps_v = taps_v_ref[...]
    decays = []
    writes = []
    for member in range(group):
        decays.append(cumulated(head_rows(decay_ref, ratio, chunks, group, member)))
        writes.append(
            lax.dot_general(
                eye,
                head_rows(write_ref, ratio, chunks, group, member),
                (((1,), (1,)), ((), ())),
                precision=EXACT,
                preferred_element_type=F32,
            )
        )
    keys = {}
    flipped = {}
    values = []
    inner = {}
    for chunk in range(chunks):
        rows = slice(chunk * CHUNK, (chunk + 1) * CHUNK)
        smoothed = conv_chunk(stage_k, taps_k, chunk)
        values.append(conv_chunk(stage_v, taps_v, chunk))
        for member in range(group):
            lanes = slice(member * HD, (member + 1) * HD)
            key = unit_rows(smoothed[:, lanes], 1.0)
            keys_out[rows, lanes] = key.astype(BF)
            keys[member, chunk] = key
            flipped[member, chunk] = key.T
            inner[member, chunk] = mm(key, flipped[member, chunk])
    units = [
        (member, head, chunk)
        for member in range(group)
        for head in range(ratio)
        for chunk in range(chunks)
    ]
    systems = []
    for member, head, chunk in units:
        at = chunk * ratio + head
        decay_rows, decay_cols = decays[member]
        fading = jnp.exp(
            jnp.minimum(decay_cols[:, at : at + 1] - decay_rows[at : at + 1], 0.0)
        )
        systems.append(
            jnp.where(
                row_ids > col_ids,
                writes[member][:, at : at + 1] * inner[member, chunk] * fading,
                0.0,
            )
        )
    inverses = inverted(systems)
    maps = {}
    for (member, head, chunk), inverse in zip(units, inverses):
        at = chunk * ratio + head
        place = member * ratio + head
        decay_rows, decay_cols = decays[member]
        col = decay_cols[:, at : at + 1]
        write = writes[member][:, at : at + 1]
        value = values[chunk][:, place * HD : (place + 1) * HD]
        right = jnp.concatenate(
            [keys[member, chunk] * (write * jnp.exp(col)), value * write], axis=1
        )
        solved = mm(inverse, right).astype(BF)
        wy_out[place, chunk * CHUNK : (chunk + 1) * CHUNK] = solved
        row = decay_rows[at : at + 1]
        end = row[:, CHUNK - 1 : CHUNK]
        maps[place, chunk] = (
            mm(flipped[member, chunk] * jnp.exp(end - row), solved),
            jnp.exp(end),
        )
    states = [None] * (group * ratio)
    for chunk in range(chunks):
        for place, state in enumerate(states):
            product, end = maps[place, chunk]
            linear = eye * end - product[:, :HD]
            added = product[:, HD:]
            if state is None:
                states[place] = jnp.concatenate([linear, added], axis=1)
            else:
                starts_out[place, chunk - 1] = state.astype(BF)
                moved = mm(linear, state)
                states[place] = jnp.concatenate([moved[:, :HD], moved[:, HD:] + added], axis=1)
    for place, state in enumerate(states):
        map_out[place] = state.astype(BF)


def output_kernel(
    group,
    ratio,
    chunks,
    at_ref,
    query_ref,
    rims_ref,
    taps_ref,
    keys_ref,
    wy_ref,
    starts_ref,
    decay_ref,
    parts_out,
    stage,
):
    row_ids, col_ids = grid_ids()
    stage_rows(stage, at_ref, rims_ref, query_ref)
    decays = [
        cumulated(head_rows(decay_ref, ratio, chunks, group, member)) for member in range(group)
    ]
    taps = taps_ref[...]
    for chunk in range(chunks):
        rows = slice(chunk * CHUNK, (chunk + 1) * CHUNK)
        smoothed = conv_chunk(stage, taps, chunk)
        places = range(group * ratio)
        queries, scores = [], []
        for member in range(group):
            lanes = slice(member * HD, (member + 1) * HD)
            queries.append(unit_rows(smoothed[:, lanes], HD ** (-0.5)))
            scores.append(mm_nt(queries[-1], keys_ref[rows, lanes]))
        if chunk > 0:
            removed = [
                mm(wy_ref[place, rows, :HD], starts_ref[place, chunk - 1]) for place in places
            ]
        for place in places:
            member, head = divmod(place, ratio)
            at = chunk * ratio + head
            decay_rows, decay_cols = decays[member]
            col = decay_cols[:, at : at + 1]
            fading = jnp.exp(jnp.minimum(col - decay_rows[at : at + 1], 0.0))
            weights = jnp.where(row_ids >= col_ids, scores[member] * fading, 0.0)
            scaled = queries[member] * jnp.exp(col)
            wy = wy_ref[place, rows]
            if chunk == 0:
                whole = mm(weights, wy)
                linear = scaled - whole[:, :HD]
                local = whole[:, HD:]
            else:
                gone = removed[place]
                left = jnp.concatenate([scaled, weights], axis=1)
                rest = jnp.concatenate(
                    [-gone[:, :HD], wy[:, HD:].astype(F32) - gone[:, HD:]], axis=1
                ).astype(BF)
                whole = mm(
                    left, jnp.concatenate([starts_ref[place, chunk - 1], rest], axis=0)
                )
                linear = whole[:, :HD]
                local = whole[:, HD:]
            parts_out[place, rows, :HD] = linear.astype(BF)
            parts_out[place, rows, HD:] = local.astype(BF)


def normed_heads(heads, swap, parts_ref, kept_ref, got_ref, gate_ref, normed_ref):
    half = heads // 2
    for head in range(heads):
        lanes = slice(head * HD, (head + 1) * HD)
        kept, got = kept_ref[head % half], got_ref[head % half]
        state = jnp.where(swap, got, kept) if head < half else jnp.where(swap, kept, got)
        attended = parts_ref[head, :, HD:].astype(F32) + mm(parts_ref[head, :, :HD], state)
        spread = lax.rsqrt(jnp.mean(attended * attended, axis=-1, keepdims=True) + 1e-06)
        normed_ref[:, lanes] = (
            attended * spread * silu(gate_ref[:, lanes].astype(F32))
        ).astype(BF)


def norm_kernel(heads, plan_ref, parts_ref, kept_ref, got_ref, gate_ref, normed_ref):
    normed_heads(heads, plan_ref[0] != 0, parts_ref, kept_ref, got_ref, gate_ref, normed_ref)


def far_kernel(
    heads, plan_ref, parts_ref, kept_ref, got_ref, gate_ref, weight_hbm, out_ref, weight, normed, sems
):
    pieces = weight.shape[0]
    depth = weight.shape[1]
    copies = [
        pltpu.make_async_copy(
            weight_hbm.at[pl.ds(at * depth, depth)], weight.at[at], sems.at[at]
        )
        for at in range(pieces)
    ]
    for copy in copies:
        copy.start()
    normed_heads(heads, plan_ref[0] != 0, parts_ref, kept_ref, got_ref, gate_ref, normed)
    total = None
    for at, copy in enumerate(copies):
        copy.wait()
        part = jnp.dot(
            normed[:, at * depth : (at + 1) * depth], weight[at], preferred_element_type=F32
        )
        total = part if total is None else total + part
    out_ref[...] = total.astype(BF)


def far_rows(plan, parts, kept, got, gate_in, w_out, length):
    heads = parts.shape[0]
    features, width = w_out.shape
    pieces = 4
    return pl.pallas_call(
        functools.partial(far_kernel, heads),
        grid_spec=pltpu.PrefetchScalarGridSpec(
            num_scalar_prefetch=1,
            grid=(1,),
            in_specs=[
                pl.BlockSpec((heads, length, 2 * HD), lambda c, plan: (0, plan[1], 0)),
                WHOLE,
                WHOLE,
                pl.BlockSpec((length, heads * HD), lambda c, plan: (plan[1], 0)),
                pl.BlockSpec(memory_space=pltpu.HBM),
            ],
            out_specs=pl.BlockSpec((length, width), lambda c, plan: (0, 0)),
            scratch_shapes=[
                pltpu.VMEM((pieces, features // pieces, width), BF),
                pltpu.VMEM((length, features), BF),
                pltpu.SemaphoreType.DMA((pieces,)),
            ],
        ),
        out_shape=jax.ShapeDtypeStruct((length, width), BF),
        compiler_params=pltpu.CompilerParams(vmem_limit_bytes=20 << 20),
        name="far",
    )(plan, in_hbm(parts), kept, got, gate_in, w_out)


def final_rows(first, count, plan, parts, kept, got, gate_in, w_out, length):
    heads = parts.shape[0]
    normed = pl.pallas_call(
        functools.partial(norm_kernel, heads),
        grid_spec=pltpu.PrefetchScalarGridSpec(
            num_scalar_prefetch=1,
            grid=(count,),
            in_specs=[
                pl.BlockSpec((heads, length, 2 * HD), lambda c, plan: (0, plan[1 + first + c], 0)),
                WHOLE,
                WHOLE,
                pl.BlockSpec((length, heads * HD), lambda c, plan: (plan[1 + first + c], 0)),
            ],
            out_specs=pl.BlockSpec((length, heads * HD), lambda c, plan: (c, 0)),
        ),
        out_shape=jax.ShapeDtypeStruct((count * length, heads * HD), BF),
        compiler_params=pltpu.CompilerParams(vmem_limit_bytes=16 << 20),
        cost_estimate=cost(
            heads * count * length, heads * count * length * HD, 8 * heads * count * length * HD
        ),
        name="normed",
    )(plan, in_hbm(parts), kept, got, gate_in)
    mixed = jnp.dot(normed, w_out, preferred_element_type=F32).astype(BF)
    return mixed.reshape(count, length, w_out.shape[1])


def exchanged(value, axis, bit):
    count = lax.axis_size(axis)
    return lax.ppermute(value, axis, [(source, source ^ bit) for source in range(count)])


def after(later, earlier):
    moved = jnp.einsum(
        "hij,hjf->hif", later[..., :HD].astype(BF), earlier.astype(BF), preferred_element_type=F32
    )
    if earlier.shape[-1] == HD:
        return moved + later[..., HD:].astype(F32)
    in_state = lax.broadcasted_iota(jnp.int32, later.shape, 2) >= HD
    return moved + jnp.where(in_state, later.astype(F32), 0.0)


def incoming_state(total, axis, covers):
    early, late = covers
    count = lax.axis_size(axis)
    index = lax.axis_index(axis)
    odd = (index & 1) != 0
    half = total.shape[0] // 2
    mine = jnp.where(odd, total[half:], total[:half])
    other = exchanged(jnp.where(odd, total[:half], total[half:]), axis, 1)
    first = jnp.where(odd, other, mine)
    second = jnp.where(odd, mine, other)
    total = after(second, first).astype(BF)
    eye = jnp.broadcast_to(jnp.eye(HD, dtype=BF), (half, HD, HD))
    before = jnp.concatenate([eye, jnp.zeros_like(eye)], axis=-1)
    bit = 2
    while 2 * bit < count:
        high = (index & bit) != 0
        other = exchanged(total, axis, bit)
        if bit == 2:
            other, early = lax.optimization_barrier((other, early))
        lower, upper = jnp.where(high, other, total), jnp.where(high, total, other)
        if 4 * bit < count:
            total = after(upper, lower).astype(BF)
        else:
            total = after(upper, lower[..., HD:]).astype(BF)
        other, _ = lax.optimization_barrier((other, total))
        if bit == 2:
            before = jnp.where(high, other, before)
        else:
            before = jnp.where(high, after(before, other).astype(BF), before)
        bit *= 2
    high = (index & bit) != 0
    state = exchanged(total[..., -HD:], axis, bit)
    reach = jnp.where(high, before[..., :HD], jnp.zeros((), BF))
    before = jnp.concatenate([reach, before[..., HD:]], axis=-1)
    passed = after(first, before).astype(BF)
    keep, send = jnp.where(odd, passed, before), jnp.where(odd, before, passed)
    late = late(early)
    state, keep, send, late = lax.optimization_barrier((state, keep, send, late))
    got = exchanged(after(send, state).astype(BF), axis, 1)
    kept = after(keep, state).astype(BF)
    return kept, got, early, late


def summed(*values):
    total = values[0].astype(F32)
    for value in values[1:]:
        total = total + value.astype(F32)
    return total.astype(BF)


def line_sum(parts, axis):
    count = lax.axis_size(axis)
    index = lax.axis_index(axis)

    def take(at):
        return lax.dynamic_index_in_dim(parts, jnp.clip(at, 0, count - 1), 0, keepdims=False)

    up = down = None
    for step in range(count - 1):
        send_up = take(count - 1 - step + index)
        send_down = take(step - (count - 1 - index))
        if up is not None:
            send_up = summed(send_up, up)
            send_down = summed(send_down, down)
        up = lax.ppermute(send_up, axis, [(z, z + 1) for z in range(step + 1)])
        down = lax.ppermute(
            send_down, axis, [(count - 1 - z, count - 2 - z) for z in range(step + 1)]
        )
    return summed(take(index), up, down)


def swapped_sum(far, rows_of, axis):
    width = far.shape[-1] // 4
    early, late = slice(0, width), slice(width, 4 * width)
    first_in = exchanged(far[:, early], axis, 1)
    passed = rows_of(1, 1, None)[0]
    far_late, passed = lax.optimization_barrier((far[:, late], passed))
    later_in = exchanged(far_late, axis, 1)
    paired = summed(passed[:, early], first_in)
    first = exchanged(paired, axis, 2)
    rest = rows_of(2, 2, paired)
    later_in, first = lax.optimization_barrier((later_in, first))
    later = exchanged(summed(passed[:, late], later_in), axis, 2)
    near = exchanged(rest[0], axis, 1)
    own = rest[1]
    return jnp.concatenate(
        [
            summed(own[:, early], near[:, early], first),
            summed(own[:, late], near[:, late], later),
        ],
        axis=-1,
    )


def shards(
    inputs,
    w_query,
    w_key,
    w_value,
    w_gate_out,
    conv_query,
    conv_key,
    conv_value,
    decay_log,
    write_rate,
    w_out,
):
    def project(weights, earlier=None):
        tokens = inputs
        if earlier is not None:
            tokens, _ = lax.optimization_barrier((inputs, earlier))
        return jnp.dot(tokens, weights, preferred_element_type=F32).astype(BF)

    proj_key = project(w_key)
    proj_value = project(w_value)
    proj_query = project(w_query, (proj_key, proj_value))
    rows = inputs.shape[0]
    key_width = proj_key.shape[1]
    key_heads = key_width // HD
    heads = proj_value.shape[1] // HD
    ratio = heads // key_heads
    chunks = rows // CHUNK
    tails = jnp.concatenate(
        [proj_key[-RIM:], proj_value[-RIM:], proj_query[-RIM:]], axis=1
    )
    count = lax.axis_size("ctx")
    rims = lax.ppermute(tails, "ctx", [(at, (at + 1) % count) for at in range(count)])
    place_ctx = lax.axis_index("ctx").reshape(1)

    group = 2 if key_heads % 2 == 0 else 1

    def cols(length, width, start=0):
        return pl.BlockSpec((length, group * width), lambda h: (0, h + start // (group * width)))

    gate_spec = pl.BlockSpec((heads, rows), lambda h: (0, 0))
    wy_spec = pl.BlockSpec((group * ratio, rows, 2 * HD), lambda h: (h, 0, 0))
    starts_spec = pl.BlockSpec((group * ratio, chunks - 1, HD, 2 * HD), lambda h: (h, 0, 0, 0))
    taps_len = conv_key.shape[0]
    keys, wy, starts, total = pl.pallas_call(
        functools.partial(local_kernel, group, ratio, chunks),
        grid=(key_heads // group,),
        in_specs=[
            SCALAR,
            cols(rows, HD),
            cols(rows, ratio * HD),
            cols(RIM, HD),
            cols(RIM, ratio * HD, key_width),
            cols(taps_len, HD),
            cols(taps_len, ratio * HD),
            gate_spec,
            gate_spec,
        ],
        out_specs=[
            cols(rows, HD),
            wy_spec,
            starts_spec,
            pl.BlockSpec((group * ratio, HD, 2 * HD), lambda h: (h, 0, 0)),
        ],
        out_shape=[
            pltpu.HBM((rows, key_width), BF),
            pltpu.HBM((heads, rows, 2 * HD), BF),
            pltpu.HBM((heads, chunks - 1, HD, 2 * HD), BF),
            jax.ShapeDtypeStruct((heads, HD, 2 * HD), BF),
        ],
        scratch_shapes=[
            pltpu.VMEM((rows + 8, group * HD), F32),
            pltpu.VMEM((rows + 8, group * ratio * HD), F32),
        ],
        compiler_params=pltpu.CompilerParams(vmem_limit_bytes=32 << 20),
        cost_estimate=cost(16 * heads * rows, 4 * heads * rows * HD, 12 * heads * rows * HD),
        name="local",
    )(place_ctx, in_hbm(proj_key), in_hbm(proj_value), rims, rims, conv_key, conv_value, decay_log, write_rate)
    parts = pl.pallas_call(
        functools.partial(output_kernel, group, ratio, chunks),
        grid=(key_heads // group,),
        in_specs=[
            SCALAR,
            cols(rows, HD),
            cols(RIM, HD, key_width + heads * HD),
            cols(taps_len, HD),
            cols(rows, HD),
            wy_spec,
            starts_spec,
            gate_spec,
        ],
        out_specs=wy_spec,
        out_shape=pltpu.HBM((heads, rows, 2 * HD), BF),
        scratch_shapes=[pltpu.VMEM((rows + 8, group * HD), F32)],
        compiler_params=pltpu.CompilerParams(vmem_limit_bytes=24 << 20),
        cost_estimate=cost(8 * heads * rows, 2 * heads * rows * HD, 12 * heads * rows * HD),
        name="outputs",
    )(place_ctx, in_hbm(proj_query), rims, conv_query, in_hbm(keys), in_hbm(wy), in_hbm(starts), decay_log)
    kept, got, parts, gate_in = incoming_state(total, "ctx", (parts, functools.partial(project, w_gate_out)))
    spread = lax.axis_size("head")
    place = lax.axis_index("head")
    length = rows // spread
    swap = lax.axis_index("ctx") & 1
    if spread == 4:
        order = [place ^ 3, place ^ 2, place ^ 1, place]
    else:
        order = list(range(spread))
    plan = jnp.stack([jnp.int32(at) for at in [swap] + order])

    def rows_of(first, amount, earlier):
        steps = plan
        if earlier is not None:
            steps, _ = lax.optimization_barrier((plan, earlier))
        return final_rows(first, amount, steps, parts, kept, got, gate_in, w_out, length)

    if spread == 4:
        far = far_rows(plan, parts, kept, got, gate_in, w_out, length)
        return swapped_sum(far, rows_of, "head")
    return line_sum(rows_of(0, spread, None), "head")


def solution(mesh):
    return jax.shard_map(
        shards,
        mesh=mesh,
        in_specs=(
            P("ctx", None),
            P(None, "head"),
            P(None, "head"),
            P(None, "head"),
            P(None, "head"),
            P(None, "head"),
            P(None, "head"),
            P(None, "head"),
            P("head", "ctx"),
            P("head", "ctx"),
            P("head", None),
        ),
        out_specs=P(("ctx", "head"), None),
        check_vma=False,
    )
```

```python
import functools

import jax
import jax.numpy as jnp
from jax import lax
from jax.experimental import pallas as pl
from jax.experimental.pallas import tpu as pltpu
from jax.sharding import PartitionSpec as P

HD = 128
CHUNK = 128
RIM = 8
BF = jnp.bfloat16
F32 = jnp.float32
EXACT = lax.Precision.HIGHEST
SCALAR = pl.BlockSpec(memory_space=pltpu.SMEM)
WHOLE = pl.BlockSpec(memory_space=pltpu.VMEM)


def cost(matmul_rows, exps, size):
    return pl.CostEstimate(
        flops=2 * HD * HD * matmul_rows, transcendentals=exps, bytes_accessed=size
    )


def in_hbm(array):
    return pltpu.with_memory_space_constraint(array, pltpu.HBM)


def mm(left, right):
    return jnp.dot(left.astype(BF), right.astype(BF), preferred_element_type=F32)


def mm_nt(left, right):
    return lax.dot_general(
        left.astype(BF), right.astype(BF), (((1,), (1,)), ((), ())), preferred_element_type=F32
    )


def silu(values):
    return values / (1.0 + jnp.exp(-values))


def unit_rows(values, factor):
    return values * (lax.rsqrt(jnp.sum(values * values, axis=-1, keepdims=True) + 1e-06) * factor)


def stage_rows(stage, at_ref, rims_ref, rows_ref):
    stage[0:8] = jnp.where(at_ref[0] > 0, rims_ref[RIM - 8 : RIM].astype(F32), 0.0)
    stage[8:] = rows_ref[...].astype(F32)


def conv_chunk(stage, taps, chunk):
    taps_len = taps.shape[0]
    start = 8 - (taps_len - 1) + chunk * CHUNK
    total = taps[0:1] * stage[start : start + CHUNK]
    for offset in range(1, taps_len):
        total = total + taps[offset : offset + 1] * stage[start + offset : start + offset + CHUNK]
    return silu(total)


def grid_ids():
    row_ids = lax.broadcasted_iota(jnp.int32, (CHUNK, CHUNK), 0)
    col_ids = lax.broadcasted_iota(jnp.int32, (CHUNK, CHUNK), 1)
    return row_ids, col_ids


def cumulated(decay):
    row_ids, col_ids = grid_ids()
    lower = jnp.where(row_ids >= col_ids, 1.0, 0.0)
    dims = (((1,), (1,)), ((), ()))
    as_rows = lax.dot_general(decay, lower, dims, precision=EXACT, preferred_element_type=F32)
    as_cols = lax.dot_general(lower, decay, dims, precision=EXACT, preferred_element_type=F32)
    return as_rows, as_cols


def head_rows(ref, ratio, chunks, group=1, member=0):
    start = (pl.program_id(0) * group + member) * ratio
    rows = [ref[pl.ds(start + head, 1), :] for head in range(ratio)]
    return jnp.concatenate(
        [
            row[:, chunk * CHUNK : (chunk + 1) * CHUNK]
            for chunk in range(chunks)
            for row in rows
        ],
        axis=0,
    )


def inverted(systems):
    row_ids, col_ids = grid_ids()
    same = row_ids // 2 == col_ids // 2
    eye = jnp.where(row_ids == col_ids, 1.0, 0.0)
    inverses = [eye - jnp.where(same, system, 0.0) for system in systems]
    size = 2
    while size < CHUNK:
        cross = (row_ids // (2 * size) == col_ids // (2 * size)) & (
            row_ids // size != col_ids // size
        )
        links = [jnp.where(cross, system, 0.0).astype(BF) for system in systems]
        halves = [inverse.astype(BF) for inverse in inverses]
        if size < 8:
            inner = [mm(link, half) for link, half in zip(links, halves)]
            outer = [mm(half, part) for half, part in zip(halves, inner)]
            inverses = [inverse - part for inverse, part in zip(inverses, outer)]
        else:
            starts = range(size, CHUNK, 2 * size)
            odd = [
                jnp.concatenate([inverse[s : s + size] for s in starts], axis=0)
                for inverse in inverses
            ]
            inner = [mm(part, link) for part, link in zip(odd, links)]
            outer = [mm(part, half) for part, half in zip(inner, halves)]
            odd = [part - update for part, update in zip(odd, outer)]
            inverses = [
                jnp.concatenate(
                    [
                        piece
                        for at, s in enumerate(starts)
                        for piece in (
                            inverse[s - size : s],
                            part[at * size : (at + 1) * size],
                        )
                    ],
                    axis=0,
                )
                for inverse, part in zip(inverses, odd)
            ]
        size *= 2
    return inverses


def local_kernel(
    group,
    ratio,
    chunks,
    at_ref,
    keys_ref,
    values_ref,
    rims_k_ref,
    rims_v_ref,
    taps_k_ref,
    taps_v_ref,
    decay_ref,
    write_ref,
    keys_out,
    wy_out,
    starts_out,
    map_out,
    stage_k,
    stage_v,
):
    row_ids, col_ids = grid_ids()
    eye = jnp.where(row_ids == col_ids, 1.0, 0.0)
    stage_rows(stage_k, at_ref, rims_k_ref, keys_ref)
    stage_rows(stage_v, at_ref, rims_v_ref, values_ref)
    taps_k = taps_k_ref[...]
    taps_v = taps_v_ref[...]
    decays = []
    writes = []
    for member in range(group):
        decays.append(cumulated(head_rows(decay_ref, ratio, chunks, group, member)))
        writes.append(
            lax.dot_general(
                eye,
                head_rows(write_ref, ratio, chunks, group, member),
                (((1,), (1,)), ((), ())),
                precision=EXACT,
                preferred_element_type=F32,
            )
        )
    keys = {}
    flipped = {}
    values = []
    inner = {}
    for chunk in range(chunks):
        rows = slice(chunk * CHUNK, (chunk + 1) * CHUNK)
        smoothed = conv_chunk(stage_k, taps_k, chunk)
        values.append(conv_chunk(stage_v, taps_v, chunk))
        for member in range(group):
            lanes = slice(member * HD, (member + 1) * HD)
            key = unit_rows(smoothed[:, lanes], 1.0)
            keys_out[rows, lanes] = key.astype(BF)
            keys[member, chunk] = key
            flipped[member, chunk] = key.T
            inner[member, chunk] = mm(key, flipped[member, chunk])
    units = [
        (member, head, chunk)
        for member in range(group)
        for head in range(ratio)
        for chunk in range(chunks)
    ]
    systems = []
    for member, head, chunk in units:
        at = chunk * ratio + head
        decay_rows, decay_cols = decays[member]
        fading = jnp.exp(
            jnp.minimum(decay_cols[:, at : at + 1] - decay_rows[at : at + 1], 0.0)
        )
        systems.append(
            jnp.where(
                row_ids > col_ids,
                writes[member][:, at : at + 1] * inner[member, chunk] * fading,
                0.0,
            )
        )
    inverses = inverted(systems)
    maps = {}
    for (member, head, chunk), inverse in zip(units, inverses):
        at = chunk * ratio + head
        place = member * ratio + head
        decay_rows, decay_cols = decays[member]
        col = decay_cols[:, at : at + 1]
        write = writes[member][:, at : at + 1]
        value = values[chunk][:, place * HD : (place + 1) * HD]
        right = jnp.concatenate(
            [keys[member, chunk] * (write * jnp.exp(col)), value * write], axis=1
        )
        solved = mm(inverse, right).astype(BF)
        wy_out[place, chunk * CHUNK : (chunk + 1) * CHUNK] = solved
        row = decay_rows[at : at + 1]
        end = row[:, CHUNK - 1 : CHUNK]
        maps[place, chunk] = (
            mm(flipped[member, chunk] * jnp.exp(end - row), solved),
            jnp.exp(end),
        )
    states = [None] * (group * ratio)
    for chunk in range(chunks):
        for place, state in enumerate(states):
            product, end = maps[place, chunk]
            linear = eye * end - product[:, :HD]
            added = product[:, HD:]
            if state is None:
                states[place] = jnp.concatenate([linear, added], axis=1)
            else:
                starts_out[place, chunk - 1] = state.astype(BF)
                moved = mm(linear, state)
                states[place] = jnp.concatenate([moved[:, :HD], moved[:, HD:] + added], axis=1)
    for place, state in enumerate(states):
        map_out[place] = state.astype(BF)


def output_kernel(
    group,
    ratio,
    chunks,
    at_ref,
    query_ref,
    rims_ref,
    taps_ref,
    keys_ref,
    wy_ref,
    starts_ref,
    decay_ref,
    parts_out,
    stage,
):
    row_ids, col_ids = grid_ids()
    stage_rows(stage, at_ref, rims_ref, query_ref)
    decays = [
        cumulated(head_rows(decay_ref, ratio, chunks, group, member)) for member in range(group)
    ]
    taps = taps_ref[...]
    for chunk in range(chunks):
        rows = slice(chunk * CHUNK, (chunk + 1) * CHUNK)
        smoothed = conv_chunk(stage, taps, chunk)
        places = range(group * ratio)
        queries, scores = [], []
        for member in range(group):
            lanes = slice(member * HD, (member + 1) * HD)
            queries.append(unit_rows(smoothed[:, lanes], HD ** (-0.5)))
            scores.append(mm_nt(queries[-1], keys_ref[rows, lanes]))
        if chunk > 0:
            removed = [
                mm(wy_ref[place, rows, :HD], starts_ref[place, chunk - 1]) for place in places
            ]
        for place in places:
            member, head = divmod(place, ratio)
            at = chunk * ratio + head
            decay_rows, decay_cols = decays[member]
            col = decay_cols[:, at : at + 1]
            fading = jnp.exp(jnp.minimum(col - decay_rows[at : at + 1], 0.0))
            weights = jnp.where(row_ids >= col_ids, scores[member] * fading, 0.0)
            scaled = queries[member] * jnp.exp(col)
            wy = wy_ref[place, rows]
            if chunk == 0:
                whole = mm(weights, wy)
                linear = scaled - whole[:, :HD]
                local = whole[:, HD:]
            else:
                gone = removed[place]
                left = jnp.concatenate([scaled, weights], axis=1)
                rest = jnp.concatenate(
                    [-gone[:, :HD], wy[:, HD:].astype(F32) - gone[:, HD:]], axis=1
                ).astype(BF)
                whole = mm(
                    left, jnp.concatenate([starts_ref[place, chunk - 1], rest], axis=0)
                )
                linear = whole[:, :HD]
                local = whole[:, HD:]
            parts_out[place, rows, :HD] = linear.astype(BF)
            parts_out[place, rows, HD:] = local.astype(BF)


def normed_heads(heads, swap, parts_ref, kept_ref, got_ref, gate_ref, normed_ref):
    half = heads // 2
    for head in range(heads):
        lanes = slice(head * HD, (head + 1) * HD)
        kept, got = kept_ref[head % half], got_ref[head % half]
        state = jnp.where(swap, got, kept) if head < half else jnp.where(swap, kept, got)
        attended = parts_ref[head, :, HD:].astype(F32) + mm(parts_ref[head, :, :HD], state)
        spread = lax.rsqrt(jnp.mean(attended * attended, axis=-1, keepdims=True) + 1e-06)
        normed_ref[:, lanes] = (
            attended * spread * silu(gate_ref[:, lanes].astype(F32))
        ).astype(BF)


def norm_kernel(heads, plan_ref, parts_ref, kept_ref, got_ref, gate_ref, normed_ref):
    normed_heads(heads, plan_ref[0] != 0, parts_ref, kept_ref, got_ref, gate_ref, normed_ref)


def far_kernel(
    heads,
    plan_ref,
    parts_ref,
    kept_ref,
    got_ref,
    gate_ref,
    weight_hbm,
    out_ref,
    normed_ref,
    weight,
    sems,
):
    pieces, depth, width = weight.shape
    copies = [
        pltpu.make_async_copy(
            weight_hbm.at[pl.ds(at * depth, depth), pl.ds(0, width)], weight.at[at], sems.at[at]
        )
        for at in range(pieces)
    ]
    for copy in copies:
        copy.start()
    normed_heads(heads, plan_ref[0] != 0, parts_ref, kept_ref, got_ref, gate_ref, normed_ref)
    total = None
    for at, copy in enumerate(copies):
        copy.wait()
        part = jnp.dot(
            normed_ref[:, at * depth : (at + 1) * depth],
            weight[at],
            preferred_element_type=F32,
        )
        total = part if total is None else total + part
    out_ref[...] = total.astype(BF)


def far_rows(plan, parts, kept, got, gate_in, w_out, length, width):
    heads = parts.shape[0]
    features = w_out.shape[0]
    pieces = 4
    return pl.pallas_call(
        functools.partial(far_kernel, heads),
        grid_spec=pltpu.PrefetchScalarGridSpec(
            num_scalar_prefetch=1,
            grid=(1,),
            in_specs=[
                pl.BlockSpec((heads, length, 2 * HD), lambda c, plan: (0, plan[1], 0)),
                WHOLE,
                WHOLE,
                pl.BlockSpec((length, heads * HD), lambda c, plan: (plan[1], 0)),
                pl.BlockSpec(memory_space=pltpu.HBM),
            ],
            out_specs=[
                pl.BlockSpec((length, width), lambda c, plan: (0, 0)),
                pl.BlockSpec((length, features), lambda c, plan: (0, 0)),
            ],
            scratch_shapes=[
                pltpu.VMEM((pieces, features // pieces, width), BF),
                pltpu.SemaphoreType.DMA((pieces,)),
            ],
        ),
        out_shape=[
            jax.ShapeDtypeStruct((length, width), BF),
            jax.ShapeDtypeStruct((length, features), BF),
        ],
        compiler_params=pltpu.CompilerParams(vmem_limit_bytes=20 << 20),
        name="far",
    )(plan, in_hbm(parts), kept, got, gate_in, w_out)


def normed_rows(first, count, plan, parts, kept, got, gate_in, length):
    heads = parts.shape[0]
    return pl.pallas_call(
        functools.partial(norm_kernel, heads),
        grid_spec=pltpu.PrefetchScalarGridSpec(
            num_scalar_prefetch=1,
            grid=(count,),
            in_specs=[
                pl.BlockSpec((heads, length, 2 * HD), lambda c, plan: (0, plan[1 + first + c], 0)),
                WHOLE,
                WHOLE,
                pl.BlockSpec((length, heads * HD), lambda c, plan: (plan[1 + first + c], 0)),
            ],
            out_specs=pl.BlockSpec((length, heads * HD), lambda c, plan: (c, 0)),
        ),
        out_shape=jax.ShapeDtypeStruct((count * length, heads * HD), BF),
        compiler_params=pltpu.CompilerParams(vmem_limit_bytes=16 << 20),
        cost_estimate=cost(
            heads * count * length, heads * count * length * HD, 8 * heads * count * length * HD
        ),
        name="normed",
    )(plan, in_hbm(parts), kept, got, gate_in)


def exchanged(value, axis, bit):
    count = lax.axis_size(axis)
    return lax.ppermute(value, axis, [(source, source ^ bit) for source in range(count)])


def after(later, earlier):
    moved = jnp.einsum(
        "hij,hjf->hif", later[..., :HD].astype(BF), earlier.astype(BF), preferred_element_type=F32
    )
    if earlier.shape[-1] == HD:
        return moved + later[..., HD:].astype(F32)
    in_state = lax.broadcasted_iota(jnp.int32, later.shape, 2) >= HD
    return moved + jnp.where(in_state, later.astype(F32), 0.0)


def incoming_state(total, axis, covers):
    early, late = covers
    count = lax.axis_size(axis)
    index = lax.axis_index(axis)
    odd = (index & 1) != 0
    half = total.shape[0] // 2
    mine = jnp.where(odd, total[half:], total[:half])
    other = exchanged(jnp.where(odd, total[:half], total[half:]), axis, 1)
    first = jnp.where(odd, other, mine)
    second = jnp.where(odd, mine, other)
    total = after(second, first).astype(BF)
    eye = jnp.broadcast_to(jnp.eye(HD, dtype=BF), (half, HD, HD))
    before = jnp.concatenate([eye, jnp.zeros_like(eye)], axis=-1)
    bit = 2
    while 2 * bit < count:
        high = (index & bit) != 0
        other = exchanged(total, axis, bit)
        if bit == 2:
            other, early = lax.optimization_barrier((other, early))
        lower, upper = jnp.where(high, other, total), jnp.where(high, total, other)
        if 4 * bit < count:
            total = after(upper, lower).astype(BF)
        else:
            total = after(upper, lower[..., HD:]).astype(BF)
        other, _ = lax.optimization_barrier((other, total))
        if bit == 2:
            before = jnp.where(high, other, before)
        else:
            before = jnp.where(high, after(before, other).astype(BF), before)
        bit *= 2
    high = (index & bit) != 0
    state = exchanged(total[..., -HD:], axis, bit)
    reach = jnp.where(high, before[..., :HD], jnp.zeros((), BF))
    before = jnp.concatenate([reach, before[..., HD:]], axis=-1)
    passed = after(first, before).astype(BF)
    keep, send = jnp.where(odd, passed, before), jnp.where(odd, before, passed)
    late = late(early)
    state, keep, send, late = lax.optimization_barrier((state, keep, send, late))
    got = exchanged(after(send, state).astype(BF), axis, 1)
    kept = after(keep, state).astype(BF)
    return kept, got, early, late


def summed(*values):
    total = values[0].astype(F32)
    for value in values[1:]:
        total = total + value.astype(F32)
    return total.astype(BF)


def line_sum(parts, axis):
    count = lax.axis_size(axis)
    index = lax.axis_index(axis)

    def take(at):
        return lax.dynamic_index_in_dim(parts, jnp.clip(at, 0, count - 1), 0, keepdims=False)

    up = down = None
    for step in range(count - 1):
        send_up = take(count - 1 - step + index)
        send_down = take(step - (count - 1 - index))
        if up is not None:
            send_up = summed(send_up, up)
            send_down = summed(send_down, down)
        up = lax.ppermute(send_up, axis, [(z, z + 1) for z in range(step + 1)])
        down = lax.ppermute(
            send_down, axis, [(count - 1 - z, count - 2 - z) for z in range(step + 1)]
        )
    return summed(take(index), up, down)


def mixed_rows(normed, w_out):
    return jnp.dot(normed, w_out, preferred_element_type=F32).astype(BF)


def swapped_sum(far, far_normed, w_out, rows_of, axis):
    width = far.shape[-1]
    early, late = slice(0, width), slice(width, w_out.shape[1])
    first_in = exchanged(far, axis, 1)
    far_normed, passed = lax.optimization_barrier((far_normed, rows_of(1, 1, far)))
    far_late = mixed_rows(far_normed, w_out)[:, late]
    later_in = exchanged(far_late, axis, 1)
    passed, _ = lax.optimization_barrier((passed, far_late))
    passed = mixed_rows(passed, w_out)
    paired = summed(passed[:, early], first_in)
    first = exchanged(paired, axis, 2)
    rest = mixed_rows(rows_of(2, 2, paired), w_out).reshape(2, -1, w_out.shape[1])
    later_in, first = lax.optimization_barrier((later_in, first))
    later = exchanged(summed(passed[:, late], later_in), axis, 2)
    near = exchanged(rest[0], axis, 1)
    own = rest[1]
    return jnp.concatenate(
        [
            summed(own[:, early], near[:, early], first),
            summed(own[:, late], near[:, late], later),
        ],
        axis=-1,
    )


def shards(
    inputs,
    w_query,
    w_key,
    w_value,
    w_gate_out,
    conv_query,
    conv_key,
    conv_value,
    decay_log,
    write_rate,
    w_out,
):
    def project(weights, earlier=None):
        tokens = inputs
        if earlier is not None:
            tokens, _ = lax.optimization_barrier((inputs, earlier))
        return jnp.dot(tokens, weights, preferred_element_type=F32).astype(BF)

    proj_key = project(w_key)
    proj_value = project(w_value)
    proj_query = project(w_query, (proj_key, proj_value))
    rows = inputs.shape[0]
    key_width = proj_key.shape[1]
    key_heads = key_width // HD
    heads = proj_value.shape[1] // HD
    ratio = heads // key_heads
    chunks = rows // CHUNK
    tails = jnp.concatenate(
        [proj_key[-RIM:], proj_value[-RIM:], proj_query[-RIM:]], axis=1
    )
    count = lax.axis_size("ctx")
    rims = lax.ppermute(tails, "ctx", [(at, (at + 1) % count) for at in range(count)])
    place_ctx = lax.axis_index("ctx").reshape(1)

    group = 2 if key_heads % 2 == 0 else 1

    def cols(length, width, start=0):
        return pl.BlockSpec((length, group * width), lambda h: (0, h + start // (group * width)))

    gate_spec = pl.BlockSpec((heads, rows), lambda h: (0, 0))
    wy_spec = pl.BlockSpec((group * ratio, rows, 2 * HD), lambda h: (h, 0, 0))
    starts_spec = pl.BlockSpec((group * ratio, chunks - 1, HD, 2 * HD), lambda h: (h, 0, 0, 0))
    taps_len = conv_key.shape[0]
    keys, wy, starts, total = pl.pallas_call(
        functools.partial(local_kernel, group, ratio, chunks),
        grid=(key_heads // group,),
        in_specs=[
            SCALAR,
            cols(rows, HD),
            cols(rows, ratio * HD),
            cols(RIM, HD),
            cols(RIM, ratio * HD, key_width),
            cols(taps_len, HD),
            cols(taps_len, ratio * HD),
            gate_spec,
            gate_spec,
        ],
        out_specs=[
            cols(rows, HD),
            wy_spec,
            starts_spec,
            pl.BlockSpec((group * ratio, HD, 2 * HD), lambda h: (h, 0, 0)),
        ],
        out_shape=[
            pltpu.HBM((rows, key_width), BF),
            pltpu.HBM((heads, rows, 2 * HD), BF),
            pltpu.HBM((heads, chunks - 1, HD, 2 * HD), BF),
            jax.ShapeDtypeStruct((heads, HD, 2 * HD), BF),
        ],
        scratch_shapes=[
            pltpu.VMEM((rows + 8, group * HD), F32),
            pltpu.VMEM((rows + 8, group * ratio * HD), F32),
        ],
        compiler_params=pltpu.CompilerParams(vmem_limit_bytes=32 << 20),
        cost_estimate=cost(16 * heads * rows, 4 * heads * rows * HD, 12 * heads * rows * HD),
        name="local",
    )(place_ctx, in_hbm(proj_key), in_hbm(proj_value), rims, rims, conv_key, conv_value, decay_log, write_rate)
    parts = pl.pallas_call(
        functools.partial(output_kernel, group, ratio, chunks),
        grid=(key_heads // group,),
        in_specs=[
            SCALAR,
            cols(rows, HD),
            cols(RIM, HD, key_width + heads * HD),
            cols(taps_len, HD),
            cols(rows, HD),
            wy_spec,
            starts_spec,
            gate_spec,
        ],
        out_specs=wy_spec,
        out_shape=pltpu.HBM((heads, rows, 2 * HD), BF),
        scratch_shapes=[pltpu.VMEM((rows + 8, group * HD), F32)],
        compiler_params=pltpu.CompilerParams(vmem_limit_bytes=24 << 20),
        cost_estimate=cost(8 * heads * rows, 2 * heads * rows * HD, 12 * heads * rows * HD),
        name="outputs",
    )(place_ctx, in_hbm(proj_query), rims, conv_query, in_hbm(keys), in_hbm(wy), in_hbm(starts), decay_log)
    kept, got, parts, gate_in = incoming_state(total, "ctx", (parts, functools.partial(project, w_gate_out)))
    spread = lax.axis_size("head")
    place = lax.axis_index("head")
    length = rows // spread
    swap = lax.axis_index("ctx") & 1
    if spread == 4:
        order = [place ^ 3, place ^ 2, place ^ 1, place]
    else:
        order = list(range(spread))
    plan = jnp.stack([jnp.int32(at) for at in [swap] + order])

    def rows_of(first, amount, earlier):
        steps = plan
        if earlier is not None:
            steps, _ = lax.optimization_barrier((plan, earlier))
        return normed_rows(first, amount, steps, parts, kept, got, gate_in, length)

    if spread == 4:
        far, far_normed = far_rows(
            plan, parts, kept, got, gate_in, w_out, length, 3 * w_out.shape[1] // 8
        )
        return swapped_sum(far, far_normed, w_out, rows_of, "head")
    whole = mixed_rows(rows_of(0, spread, None), w_out)
    return line_sum(whole.reshape(spread, length, w_out.shape[1]), "head")


def solution(mesh):
    return jax.shard_map(
        shards,
        mesh=mesh,
        in_specs=(
            P("ctx", None),
            P(None, "head"),
            P(None, "head"),
            P(None, "head"),
            P(None, "head"),
            P(None, "head"),
            P(None, "head"),
            P(None, "head"),
            P("head", "ctx"),
            P("head", "ctx"),
            P("head", None),
        ),
        out_specs=P(("ctx", "head"), None),
        check_vma=False,
    )
```

```python
import functools

import jax
import jax.numpy as jnp
from jax import lax
from jax.experimental import pallas as pl
from jax.experimental.pallas import tpu as pltpu
from jax.sharding import PartitionSpec as P

HD = 128
CHUNK = 128
RIM = 8
BF = jnp.bfloat16
F32 = jnp.float32
EXACT = lax.Precision.HIGHEST
SCALAR = pl.BlockSpec(memory_space=pltpu.SMEM)
WHOLE = pl.BlockSpec(memory_space=pltpu.VMEM)


def cost(matmul_rows, exps, size):
    return pl.CostEstimate(
        flops=2 * HD * HD * matmul_rows, transcendentals=exps, bytes_accessed=size
    )


def in_hbm(array):
    return pltpu.with_memory_space_constraint(array, pltpu.HBM)


def mm(left, right):
    return jnp.dot(left.astype(BF), right.astype(BF), preferred_element_type=F32)


def mm_nt(left, right):
    return lax.dot_general(
        left.astype(BF), right.astype(BF), (((1,), (1,)), ((), ())), preferred_element_type=F32
    )


def silu(values):
    return values / (1.0 + jnp.exp(-values))


def unit_rows(values, factor):
    return values * (lax.rsqrt(jnp.sum(values * values, axis=-1, keepdims=True) + 1e-06) * factor)


def stage_rows(stage, at_ref, rims_ref, rows_ref):
    stage[0:8] = jnp.where(at_ref[0] > 0, rims_ref[RIM - 8 : RIM].astype(F32), 0.0)
    stage[8:] = rows_ref[...].astype(F32)


def conv_chunk(stage, taps, chunk):
    taps_len = taps.shape[0]
    start = 8 - (taps_len - 1) + chunk * CHUNK
    total = taps[0:1] * stage[start : start + CHUNK]
    for offset in range(1, taps_len):
        total = total + taps[offset : offset + 1] * stage[start + offset : start + offset + CHUNK]
    return silu(total)


def grid_ids():
    row_ids = lax.broadcasted_iota(jnp.int32, (CHUNK, CHUNK), 0)
    col_ids = lax.broadcasted_iota(jnp.int32, (CHUNK, CHUNK), 1)
    return row_ids, col_ids


def cumulated(decay):
    row_ids, col_ids = grid_ids()
    lower = jnp.where(row_ids >= col_ids, 1.0, 0.0)
    as_rows = lax.dot_general(
        decay, lower, (((1,), (1,)), ((), ())), precision=EXACT, preferred_element_type=F32
    )
    return as_rows, as_rows.T


def head_rows(ref, ratio, chunks, group=1, member=0):
    start = (pl.program_id(0) * group + member) * ratio
    rows = [ref[pl.ds(start + head, 1), :] for head in range(ratio)]
    return jnp.concatenate(
        [
            row[:, chunk * CHUNK : (chunk + 1) * CHUNK]
            for chunk in range(chunks)
            for row in rows
        ],
        axis=0,
    )


def inverted(systems):
    row_ids, col_ids = grid_ids()
    same = row_ids // 2 == col_ids // 2
    eye = jnp.where(row_ids == col_ids, 1.0, 0.0)
    inverses = [eye - jnp.where(same, system, 0.0) for system in systems]
    size = 2
    while size < CHUNK:
        cross = (row_ids // (2 * size) == col_ids // (2 * size)) & (
            row_ids // size != col_ids // size
        )
        links = [jnp.where(cross, system, 0.0).astype(BF) for system in systems]
        halves = [inverse.astype(BF) for inverse in inverses]
        if size < 8:
            inner = [mm(link, half) for link, half in zip(links, halves)]
            outer = [mm(half, part) for half, part in zip(halves, inner)]
            inverses = [inverse - part for inverse, part in zip(inverses, outer)]
        else:
            starts = range(size, CHUNK, 2 * size)
            odd = [
                jnp.concatenate([inverse[s : s + size] for s in starts], axis=0)
                for inverse in inverses
            ]
            inner = [mm(part, link) for part, link in zip(odd, links)]
            outer = [mm(part, half) for part, half in zip(inner, halves)]
            odd = [part - update for part, update in zip(odd, outer)]
            inverses = [
                jnp.concatenate(
                    [
                        piece
                        for at, s in enumerate(starts)
                        for piece in (
                            inverse[s - size : s],
                            part[at * size : (at + 1) * size],
                        )
                    ],
                    axis=0,
                )
                for inverse, part in zip(inverses, odd)
            ]
        size *= 2
    return inverses


def local_kernel(
    group,
    ratio,
    chunks,
    at_ref,
    keys_ref,
    values_ref,
    rims_k_ref,
    rims_v_ref,
    taps_k_ref,
    taps_v_ref,
    decay_ref,
    write_ref,
    keys_out,
    wy_out,
    starts_out,
    map_out,
    stage_k,
    stage_v,
):
    row_ids, col_ids = grid_ids()
    eye = jnp.where(row_ids == col_ids, 1.0, 0.0)
    stage_rows(stage_k, at_ref, rims_k_ref, keys_ref)
    stage_rows(stage_v, at_ref, rims_v_ref, values_ref)
    taps_k = taps_k_ref[...]
    taps_v = taps_v_ref[...]
    decays = []
    writes = []
    for member in range(group):
        decays.append(cumulated(head_rows(decay_ref, ratio, chunks, group, member)))
        writes.append(head_rows(write_ref, ratio, chunks, group, member).T)
    keys = {}
    flipped = {}
    values = []
    inner = {}
    for chunk in range(chunks):
        rows = slice(chunk * CHUNK, (chunk + 1) * CHUNK)
        smoothed = conv_chunk(stage_k, taps_k, chunk)
        values.append(conv_chunk(stage_v, taps_v, chunk))
        for member in range(group):
            lanes = slice(member * HD, (member + 1) * HD)
            key = unit_rows(smoothed[:, lanes], 1.0)
            keys_out[rows, lanes] = key.astype(BF)
            keys[member, chunk] = key
            flipped[member, chunk] = key.T
            inner[member, chunk] = mm(key, flipped[member, chunk])
    units = [
        (member, head, chunk)
        for member in range(group)
        for head in range(ratio)
        for chunk in range(chunks)
    ]
    systems = []
    for member, head, chunk in units:
        at = chunk * ratio + head
        decay_rows, decay_cols = decays[member]
        fading = jnp.exp(
            jnp.minimum(decay_cols[:, at : at + 1] - decay_rows[at : at + 1], 0.0)
        )
        systems.append(
            jnp.where(
                row_ids > col_ids,
                writes[member][:, at : at + 1] * inner[member, chunk] * fading,
                0.0,
            )
        )
    inverses = inverted(systems)
    maps = {}
    for (member, head, chunk), inverse in zip(units, inverses):
        at = chunk * ratio + head
        place = member * ratio + head
        decay_rows, decay_cols = decays[member]
        col = decay_cols[:, at : at + 1]
        write = writes[member][:, at : at + 1]
        value = values[chunk][:, place * HD : (place + 1) * HD]
        right = jnp.concatenate(
            [keys[member, chunk] * (write * jnp.exp(col)), value * write], axis=1
        )
        solved = mm(inverse, right).astype(BF)
        wy_out[place, chunk * CHUNK : (chunk + 1) * CHUNK] = solved
        row = decay_rows[at : at + 1]
        end = row[:, CHUNK - 1 : CHUNK]
        maps[place, chunk] = (
            mm(flipped[member, chunk] * jnp.exp(end - row), solved),
            jnp.exp(end),
        )
    states = [None] * (group * ratio)
    for chunk in range(chunks):
        for place, state in enumerate(states):
            product, end = maps[place, chunk]
            removed, added = product[:, :HD], product[:, HD:]
            if state is None:
                states[place] = jnp.concatenate([eye * end - removed, added], axis=1)
            else:
                starts_out[place, chunk - 1] = state.astype(BF)
                moved = end * state - mm(removed, state)
                states[place] = jnp.concatenate([moved[:, :HD], moved[:, HD:] + added], axis=1)
    for place, state in enumerate(states):
        map_out[place] = state.astype(BF)


def output_kernel(
    group,
    ratio,
    chunks,
    at_ref,
    query_ref,
    rims_ref,
    taps_ref,
    keys_ref,
    wy_ref,
    starts_ref,
    decay_ref,
    parts_out,
    stage,
):
    row_ids, col_ids = grid_ids()
    stage_rows(stage, at_ref, rims_ref, query_ref)
    decays = [
        cumulated(head_rows(decay_ref, ratio, chunks, group, member)) for member in range(group)
    ]
    taps = taps_ref[...]
    for chunk in range(chunks):
        rows = slice(chunk * CHUNK, (chunk + 1) * CHUNK)
        smoothed = conv_chunk(stage, taps, chunk)
        places = range(group * ratio)
        queries, scores = [], []
        for member in range(group):
            lanes = slice(member * HD, (member + 1) * HD)
            queries.append(unit_rows(smoothed[:, lanes], HD ** (-0.5)))
            scores.append(mm_nt(queries[-1], keys_ref[rows, lanes]))
        if chunk > 0:
            removed = [
                mm(wy_ref[place, rows, :HD], starts_ref[place, chunk - 1]) for place in places
            ]
        for place in places:
            member, head = divmod(place, ratio)
            at = chunk * ratio + head
            decay_rows, decay_cols = decays[member]
            col = decay_cols[:, at : at + 1]
            fading = jnp.exp(jnp.minimum(col - decay_rows[at : at + 1], 0.0))
            weights = jnp.where(row_ids >= col_ids, scores[member] * fading, 0.0)
            scaled = queries[member] * jnp.exp(col)
            wy = wy_ref[place, rows]
            if chunk == 0:
                whole = mm(weights, wy)
                linear = scaled - whole[:, :HD]
                local = whole[:, HD:]
            else:
                gone = removed[place]
                left = jnp.concatenate([scaled, weights], axis=1)
                rest = jnp.concatenate(
                    [-gone[:, :HD], wy[:, HD:].astype(F32) - gone[:, HD:]], axis=1
                ).astype(BF)
                whole = mm(
                    left, jnp.concatenate([starts_ref[place, chunk - 1], rest], axis=0)
                )
                linear = whole[:, :HD]
                local = whole[:, HD:]
            parts_out[place, rows, :HD] = linear.astype(BF)
            parts_out[place, rows, HD:] = local.astype(BF)


def normed_heads(heads, swap, parts_ref, kept_ref, got_ref, gate_ref, normed_ref):
    half = heads // 2
    for head in range(heads):
        lanes = slice(head * HD, (head + 1) * HD)
        kept, got = kept_ref[head % half], got_ref[head % half]
        state = jnp.where(swap, got, kept) if head < half else jnp.where(swap, kept, got)
        attended = parts_ref[head, :, HD:].astype(F32) + mm(parts_ref[head, :, :HD], state)
        spread = lax.rsqrt(jnp.mean(attended * attended, axis=-1, keepdims=True) + 1e-06)
        normed_ref[:, lanes] = (
            attended * spread * silu(gate_ref[:, lanes].astype(F32))
        ).astype(BF)


def norm_kernel(heads, plan_ref, parts_ref, kept_ref, got_ref, gate_ref, normed_ref):
    normed_heads(heads, plan_ref[0] != 0, parts_ref, kept_ref, got_ref, gate_ref, normed_ref)


def far_kernel(
    heads,
    plan_ref,
    parts_ref,
    kept_ref,
    got_ref,
    gate_ref,
    weight_hbm,
    out_ref,
    normed_ref,
    weight,
    sems,
):
    pieces, depth, width = weight.shape
    copies = [
        pltpu.make_async_copy(
            weight_hbm.at[pl.ds(at * depth, depth), pl.ds(0, width)], weight.at[at], sems.at[at]
        )
        for at in range(pieces)
    ]
    for copy in copies:
        copy.start()
    normed_heads(heads, plan_ref[0] != 0, parts_ref, kept_ref, got_ref, gate_ref, normed_ref)
    total = None
    for at, copy in enumerate(copies):
        copy.wait()
        part = jnp.dot(
            normed_ref[:, at * depth : (at + 1) * depth],
            weight[at],
            preferred_element_type=F32,
        )
        total = part if total is None else total + part
    out_ref[...] = total.astype(BF)


def far_rows(plan, parts, kept, got, gate_in, w_out, length, width):
    heads = parts.shape[0]
    features = w_out.shape[0]
    pieces = 4
    return pl.pallas_call(
        functools.partial(far_kernel, heads),
        grid_spec=pltpu.PrefetchScalarGridSpec(
            num_scalar_prefetch=1,
            grid=(1,),
            in_specs=[
                pl.BlockSpec((heads, length, 2 * HD), lambda c, plan: (0, plan[1], 0)),
                WHOLE,
                WHOLE,
                pl.BlockSpec((length, heads * HD), lambda c, plan: (plan[1], 0)),
                pl.BlockSpec(memory_space=pltpu.HBM),
            ],
            out_specs=[
                pl.BlockSpec((length, width), lambda c, plan: (0, 0)),
                pl.BlockSpec((length, features), lambda c, plan: (0, 0)),
            ],
            scratch_shapes=[
                pltpu.VMEM((pieces, features // pieces, width), BF),
                pltpu.SemaphoreType.DMA((pieces,)),
            ],
        ),
        out_shape=[
            jax.ShapeDtypeStruct((length, width), BF),
            jax.ShapeDtypeStruct((length, features), BF),
        ],
        compiler_params=pltpu.CompilerParams(vmem_limit_bytes=20 << 20),
        name="far",
    )(plan, in_hbm(parts), kept, got, gate_in, w_out)


def normed_rows(first, count, plan, parts, kept, got, gate_in, length):
    heads = parts.shape[0]
    return pl.pallas_call(
        functools.partial(norm_kernel, heads),
        grid_spec=pltpu.PrefetchScalarGridSpec(
            num_scalar_prefetch=1,
            grid=(count,),
            in_specs=[
                pl.BlockSpec((heads, length, 2 * HD), lambda c, plan: (0, plan[1 + first + c], 0)),
                WHOLE,
                WHOLE,
                pl.BlockSpec((length, heads * HD), lambda c, plan: (plan[1 + first + c], 0)),
            ],
            out_specs=pl.BlockSpec((length, heads * HD), lambda c, plan: (c, 0)),
        ),
        out_shape=jax.ShapeDtypeStruct((count * length, heads * HD), BF),
        compiler_params=pltpu.CompilerParams(vmem_limit_bytes=16 << 20),
        cost_estimate=cost(
            heads * count * length, heads * count * length * HD, 8 * heads * count * length * HD
        ),
        name="normed",
    )(plan, in_hbm(parts), kept, got, gate_in)


def exchanged(value, axis, bit):
    count = lax.axis_size(axis)
    return lax.ppermute(value, axis, [(source, source ^ bit) for source in range(count)])


def after(later, earlier):
    moved = jnp.einsum(
        "hij,hjf->hif", later[..., :HD].astype(BF), earlier.astype(BF), preferred_element_type=F32
    )
    if earlier.shape[-1] == HD:
        return moved + later[..., HD:].astype(F32)
    in_state = lax.broadcasted_iota(jnp.int32, later.shape, 2) >= HD
    return moved + jnp.where(in_state, later.astype(F32), 0.0)


def incoming_state(total, axis, covers):
    early, late = covers
    count = lax.axis_size(axis)
    index = lax.axis_index(axis)
    odd = (index & 1) != 0
    half = total.shape[0] // 2
    mine = jnp.where(odd, total[half:], total[:half])
    other = exchanged(jnp.where(odd, total[:half], total[half:]), axis, 1)
    first = jnp.where(odd, other, mine)
    second = jnp.where(odd, mine, other)
    total = after(second, first).astype(BF)
    eye = jnp.broadcast_to(jnp.eye(HD, dtype=BF), (half, HD, HD))
    before = jnp.concatenate([eye, jnp.zeros_like(eye)], axis=-1)
    bit = 2
    while 2 * bit < count:
        high = (index & bit) != 0
        other = exchanged(total, axis, bit)
        if bit == 2:
            other, early = lax.optimization_barrier((other, early))
        lower, upper = jnp.where(high, other, total), jnp.where(high, total, other)
        if 4 * bit < count:
            total = after(upper, lower).astype(BF)
        else:
            total = after(upper, lower[..., HD:]).astype(BF)
        other, _ = lax.optimization_barrier((other, total))
        if bit == 2:
            before = jnp.where(high, other, before)
        else:
            before = jnp.where(high, after(before, other).astype(BF), before)
        bit *= 2
    high = (index & bit) != 0
    state = exchanged(total[..., -HD:], axis, bit)
    reach = jnp.where(high, before[..., :HD], jnp.zeros((), BF))
    before = jnp.concatenate([reach, before[..., HD:]], axis=-1)
    passed = after(first, before).astype(BF)
    keep, send = jnp.where(odd, passed, before), jnp.where(odd, before, passed)
    late = late(early)
    state, keep, send, late = lax.optimization_barrier((state, keep, send, late))
    got = exchanged(after(send, state).astype(BF), axis, 1)
    kept = after(keep, state).astype(BF)
    return kept, got, early, late


def summed(*values):
    total = values[0].astype(F32)
    for value in values[1:]:
        total = total + value.astype(F32)
    return total.astype(BF)


def line_sum(parts, axis):
    count = lax.axis_size(axis)
    index = lax.axis_index(axis)

    def take(at):
        return lax.dynamic_index_in_dim(parts, jnp.clip(at, 0, count - 1), 0, keepdims=False)

    up = down = None
    for step in range(count - 1):
        send_up = take(count - 1 - step + index)
        send_down = take(step - (count - 1 - index))
        if up is not None:
            send_up = summed(send_up, up)
            send_down = summed(send_down, down)
        up = lax.ppermute(send_up, axis, [(z, z + 1) for z in range(step + 1)])
        down = lax.ppermute(
            send_down, axis, [(count - 1 - z, count - 2 - z) for z in range(step + 1)]
        )
    return summed(take(index), up, down)


def mixed_rows(normed, w_out):
    return jnp.dot(normed, w_out, preferred_element_type=F32).astype(BF)


def swapped_sum(far, far_normed, w_out, rows_of, axis):
    width = far.shape[-1]
    early, late = slice(0, width), slice(width, w_out.shape[1])
    first_in = exchanged(far, axis, 1)
    far_normed, passed = lax.optimization_barrier((far_normed, rows_of(1, 1, far)))
    far_late = mixed_rows(far_normed, w_out)[:, late]
    later_in = exchanged(far_late, axis, 1)
    passed, _ = lax.optimization_barrier((passed, far_late))
    passed = mixed_rows(passed, w_out)
    paired = summed(passed[:, early], first_in)
    first = exchanged(paired, axis, 2)
    rest = mixed_rows(rows_of(2, 2, paired), w_out).reshape(2, -1, w_out.shape[1])
    later_in, first = lax.optimization_barrier((later_in, first))
    later = exchanged(summed(passed[:, late], later_in), axis, 2)
    near = exchanged(rest[0], axis, 1)
    own = rest[1]
    return jnp.concatenate(
        [
            summed(own[:, early], near[:, early], first),
            summed(own[:, late], near[:, late], later),
        ],
        axis=-1,
    )


def shards(
    inputs,
    w_query,
    w_key,
    w_value,
    w_gate_out,
    conv_query,
    conv_key,
    conv_value,
    decay_log,
    write_rate,
    w_out,
):
    def project(weights, earlier=None):
        tokens = inputs
        if earlier is not None:
            tokens, _ = lax.optimization_barrier((inputs, earlier))
        return jnp.dot(tokens, weights, preferred_element_type=F32).astype(BF)

    proj_key = project(w_key)
    proj_value = project(w_value)
    proj_query = project(w_query, (proj_key, proj_value))
    rows = inputs.shape[0]
    key_width = proj_key.shape[1]
    key_heads = key_width // HD
    heads = proj_value.shape[1] // HD
    ratio = heads // key_heads
    chunks = rows // CHUNK
    tails = jnp.concatenate(
        [proj_value[-RIM:], proj_key[-RIM:], proj_query[-RIM:]], axis=1
    )
    count = lax.axis_size("ctx")
    rims = lax.ppermute(tails, "ctx", [(at, (at + 1) % count) for at in range(count)])
    place_ctx = lax.axis_index("ctx").reshape(1)

    group = 2 if key_heads % 2 == 0 else 1

    def cols(length, width, start=0):
        return pl.BlockSpec((length, group * width), lambda h: (0, h + start // (group * width)))

    gate_spec = pl.BlockSpec((heads, rows), lambda h: (0, 0))
    wy_spec = pl.BlockSpec((group * ratio, rows, 2 * HD), lambda h: (h, 0, 0))
    starts_spec = pl.BlockSpec((group * ratio, chunks - 1, HD, 2 * HD), lambda h: (h, 0, 0, 0))
    taps_len = conv_key.shape[0]
    keys, wy, starts, total = pl.pallas_call(
        functools.partial(local_kernel, group, ratio, chunks),
        grid=(key_heads // group,),
        in_specs=[
            SCALAR,
            cols(rows, HD),
            cols(rows, ratio * HD),
            cols(RIM, HD, heads * HD),
            cols(RIM, ratio * HD),
            cols(taps_len, HD),
            cols(taps_len, ratio * HD),
            gate_spec,
            gate_spec,
        ],
        out_specs=[
            cols(rows, HD),
            wy_spec,
            starts_spec,
            pl.BlockSpec((group * ratio, HD, 2 * HD), lambda h: (h, 0, 0)),
        ],
        out_shape=[
            pltpu.HBM((rows, key_width), BF),
            pltpu.HBM((heads, rows, 2 * HD), BF),
            pltpu.HBM((heads, chunks - 1, HD, 2 * HD), BF),
            jax.ShapeDtypeStruct((heads, HD, 2 * HD), BF),
        ],
        scratch_shapes=[
            pltpu.VMEM((rows + 8, group * HD), F32),
            pltpu.VMEM((rows + 8, group * ratio * HD), F32),
        ],
        compiler_params=pltpu.CompilerParams(vmem_limit_bytes=32 << 20),
        cost_estimate=cost(16 * heads * rows, 4 * heads * rows * HD, 12 * heads * rows * HD),
        name="local",
    )(place_ctx, in_hbm(proj_key), in_hbm(proj_value), rims, rims, conv_key, conv_value, decay_log, write_rate)
    parts = pl.pallas_call(
        functools.partial(output_kernel, group, ratio, chunks),
        grid=(key_heads // group,),
        in_specs=[
            SCALAR,
            cols(rows, HD),
            cols(RIM, HD, key_width + heads * HD),
            cols(taps_len, HD),
            cols(rows, HD),
            wy_spec,
            starts_spec,
            gate_spec,
        ],
        out_specs=wy_spec,
        out_shape=pltpu.HBM((heads, rows, 2 * HD), BF),
        scratch_shapes=[pltpu.VMEM((rows + 8, group * HD), F32)],
        compiler_params=pltpu.CompilerParams(vmem_limit_bytes=24 << 20),
        cost_estimate=cost(8 * heads * rows, 2 * heads * rows * HD, 12 * heads * rows * HD),
        name="outputs",
    )(place_ctx, in_hbm(proj_query), rims, conv_query, in_hbm(keys), in_hbm(wy), in_hbm(starts), decay_log)
    kept, got, parts, gate_in = incoming_state(total, "ctx", (parts, functools.partial(project, w_gate_out)))
    spread = lax.axis_size("head")
    place = lax.axis_index("head")
    length = rows // spread
    swap = lax.axis_index("ctx") & 1
    if spread == 4:
        order = [place ^ 3, place ^ 2, place ^ 1, place]
    else:
        order = list(range(spread))
    plan = jnp.stack([jnp.int32(at) for at in [swap] + order])

    def rows_of(first, amount, earlier):
        steps = plan
        if earlier is not None:
            steps, _ = lax.optimization_barrier((plan, earlier))
        return normed_rows(first, amount, steps, parts, kept, got, gate_in, length)

    if spread == 4:
        far, far_normed = far_rows(
            plan, parts, kept, got, gate_in, w_out, length, 3 * w_out.shape[1] // 8
        )
        return swapped_sum(far, far_normed, w_out, rows_of, "head")
    whole = mixed_rows(rows_of(0, spread, None), w_out)
    return line_sum(whole.reshape(spread, length, w_out.shape[1]), "head")


def solution(mesh):
    return jax.shard_map(
        shards,
        mesh=mesh,
        in_specs=(
            P("ctx", None),
            P(None, "head"),
            P(None, "head"),
            P(None, "head"),
            P(None, "head"),
            P(None, "head"),
            P(None, "head"),
            P(None, "head"),
            P("head", "ctx"),
            P("head", "ctx"),
            P("head", None),
        ),
        out_specs=P(("ctx", "head"), None),
        check_vma=False,
    )
```

```python
import functools

import jax
import jax.numpy as jnp
from jax import lax
from jax.experimental import pallas as pl
from jax.experimental.pallas import tpu as pltpu
from jax.sharding import PartitionSpec as P

HD = 128
CHUNK = 128
RIM = 8
BF = jnp.bfloat16
F32 = jnp.float32
EXACT = lax.Precision.HIGHEST
SCALAR = pl.BlockSpec(memory_space=pltpu.SMEM)
WHOLE = pl.BlockSpec(memory_space=pltpu.VMEM)


def cost(matmul_rows, exps, size):
    return pl.CostEstimate(
        flops=2 * HD * HD * matmul_rows, transcendentals=exps, bytes_accessed=size
    )


def in_hbm(array):
    return pltpu.with_memory_space_constraint(array, pltpu.HBM)


def mm(left, right):
    return jnp.dot(left.astype(BF), right.astype(BF), preferred_element_type=F32)


def mm_nt(left, right):
    return lax.dot_general(
        left.astype(BF), right.astype(BF), (((1,), (1,)), ((), ())), preferred_element_type=F32
    )


def silu(values):
    return values / (1.0 + jnp.exp(-values))


def unit_rows(values, factor):
    return values * (lax.rsqrt(jnp.sum(values * values, axis=-1, keepdims=True) + 1e-06) * factor)


def stage_rows(stage, at_ref, rims_ref, rows_ref):
    stage[0:8] = jnp.where(at_ref[0] > 0, rims_ref[RIM - 8 : RIM].astype(F32), 0.0)
    stage[8:] = rows_ref[...].astype(F32)


def conv_chunk(stage, taps, chunk):
    taps_len = taps.shape[0]
    start = 8 - (taps_len - 1) + chunk * CHUNK
    total = taps[0:1] * stage[start : start + CHUNK]
    for offset in range(1, taps_len):
        total = total + taps[offset : offset + 1] * stage[start + offset : start + offset + CHUNK]
    return silu(total)


def grid_ids():
    row_ids = lax.broadcasted_iota(jnp.int32, (CHUNK, CHUNK), 0)
    col_ids = lax.broadcasted_iota(jnp.int32, (CHUNK, CHUNK), 1)
    return row_ids, col_ids


def cumulated(decay):
    row_ids, col_ids = grid_ids()
    lower = jnp.where(row_ids >= col_ids, 1.0, 0.0)
    as_rows = lax.dot_general(
        decay, lower, (((1,), (1,)), ((), ())), precision=EXACT, preferred_element_type=F32
    )
    return as_rows, as_rows.T


def head_rows(ref, ratio, chunks, group=1, member=0):
    start = (pl.program_id(0) * group + member) * ratio
    rows = [ref[pl.ds(start + head, 1), :] for head in range(ratio)]
    return jnp.concatenate(
        [
            row[:, chunk * CHUNK : (chunk + 1) * CHUNK]
            for chunk in range(chunks)
            for row in rows
        ],
        axis=0,
    )


def inverted(systems):
    row_ids, col_ids = grid_ids()
    same = row_ids // 2 == col_ids // 2
    eye = jnp.where(row_ids == col_ids, 1.0, 0.0)
    inverses = [eye - jnp.where(same, system, 0.0) for system in systems]
    size = 2
    while size < CHUNK:
        cross = (row_ids // (2 * size) == col_ids // (2 * size)) & (
            row_ids // size != col_ids // size
        )
        links = [jnp.where(cross, system, 0.0).astype(BF) for system in systems]
        halves = [inverse.astype(BF) for inverse in inverses]
        if size < 8:
            inner = [mm(link, half) for link, half in zip(links, halves)]
            outer = [mm(half, part) for half, part in zip(halves, inner)]
            inverses = [inverse - part for inverse, part in zip(inverses, outer)]
        else:
            starts = range(size, CHUNK, 2 * size)
            odd = [
                jnp.concatenate([inverse[s : s + size] for s in starts], axis=0)
                for inverse in inverses
            ]
            inner = [mm(part, link) for part, link in zip(odd, links)]
            outer = [mm(part, half) for part, half in zip(inner, halves)]
            odd = [part - update for part, update in zip(odd, outer)]
            inverses = [
                jnp.concatenate(
                    [
                        piece
                        for at, s in enumerate(starts)
                        for piece in (
                            inverse[s - size : s],
                            part[at * size : (at + 1) * size],
                        )
                    ],
                    axis=0,
                )
                for inverse, part in zip(inverses, odd)
            ]
        size *= 2
    return inverses


def local_kernel(
    group,
    ratio,
    chunks,
    at_ref,
    keys_ref,
    values_ref,
    rims_k_ref,
    rims_v_ref,
    taps_k_ref,
    taps_v_ref,
    decay_ref,
    write_ref,
    keys_out,
    wy_out,
    starts_out,
    map_out,
    stage_k,
    stage_v,
):
    row_ids, col_ids = grid_ids()
    eye = jnp.where(row_ids == col_ids, 1.0, 0.0)
    stage_rows(stage_k, at_ref, rims_k_ref, keys_ref)
    stage_rows(stage_v, at_ref, rims_v_ref, values_ref)
    taps_k = taps_k_ref[...]
    taps_v = taps_v_ref[...]
    decays = []
    writes = []
    for member in range(group):
        decays.append(cumulated(head_rows(decay_ref, ratio, chunks, group, member)))
        writes.append(head_rows(write_ref, ratio, chunks, group, member).T)
    keys = {}
    flipped = {}
    values = []
    inner = {}
    for chunk in range(chunks):
        rows = slice(chunk * CHUNK, (chunk + 1) * CHUNK)
        smoothed = conv_chunk(stage_k, taps_k, chunk)
        values.append(conv_chunk(stage_v, taps_v, chunk))
        for member in range(group):
            lanes = slice(member * HD, (member + 1) * HD)
            key = unit_rows(smoothed[:, lanes], 1.0)
            keys_out[rows, lanes] = key.astype(BF)
            keys[member, chunk] = key
            flipped[member, chunk] = key.T
            inner[member, chunk] = mm(key, flipped[member, chunk])
    units = [
        (member, head, chunk)
        for member in range(group)
        for head in range(ratio)
        for chunk in range(chunks)
    ]
    systems = []
    for member, head, chunk in units:
        at = chunk * ratio + head
        decay_rows, decay_cols = decays[member]
        fading = jnp.exp(
            jnp.minimum(decay_cols[:, at : at + 1] - decay_rows[at : at + 1], 0.0)
        )
        systems.append(
            jnp.where(
                row_ids > col_ids,
                writes[member][:, at : at + 1] * inner[member, chunk] * fading,
                0.0,
            )
        )
    inverses = inverted(systems)
    maps = {}
    for (member, head, chunk), inverse in zip(units, inverses):
        at = chunk * ratio + head
        place = member * ratio + head
        decay_rows, decay_cols = decays[member]
        col = decay_cols[:, at : at + 1]
        write = writes[member][:, at : at + 1]
        value = values[chunk][:, place * HD : (place + 1) * HD]
        right = jnp.concatenate(
            [keys[member, chunk] * (write * jnp.exp(col)), value * write], axis=1
        )
        solved = mm(inverse, right).astype(BF)
        wy_out[place, chunk * CHUNK : (chunk + 1) * CHUNK] = solved
        row = decay_rows[at : at + 1]
        end = row[:, CHUNK - 1 : CHUNK]
        maps[place, chunk] = (
            mm(flipped[member, chunk] * jnp.exp(end - row), solved),
            jnp.exp(end),
        )
    states = [None] * (group * ratio)
    for chunk in range(chunks):
        for place, state in enumerate(states):
            product, end = maps[place, chunk]
            removed, added = product[:, :HD], product[:, HD:]
            if state is None:
                states[place] = jnp.concatenate([eye * end - removed, added], axis=1)
            else:
                starts_out[place, chunk - 1] = state.astype(BF)
                moved = end * state - mm(removed, state)
                states[place] = jnp.concatenate([moved[:, :HD], moved[:, HD:] + added], axis=1)
    for place, state in enumerate(states):
        map_out[place] = state.astype(BF)


def output_kernel(
    group,
    ratio,
    chunks,
    at_ref,
    query_ref,
    rims_ref,
    taps_ref,
    keys_ref,
    wy_ref,
    starts_ref,
    decay_ref,
    parts_out,
    stage,
):
    row_ids, col_ids = grid_ids()
    stage_rows(stage, at_ref, rims_ref, query_ref)
    decays = [
        cumulated(head_rows(decay_ref, ratio, chunks, group, member)) for member in range(group)
    ]
    taps = taps_ref[...]
    for chunk in range(chunks):
        rows = slice(chunk * CHUNK, (chunk + 1) * CHUNK)
        smoothed = conv_chunk(stage, taps, chunk)
        places = range(group * ratio)
        queries, scores = [], []
        for member in range(group):
            lanes = slice(member * HD, (member + 1) * HD)
            queries.append(unit_rows(smoothed[:, lanes], HD ** (-0.5)))
            scores.append(mm_nt(queries[-1], keys_ref[rows, lanes]))
        if chunk > 0:
            removed = [
                mm(wy_ref[place, rows, :HD], starts_ref[place, chunk - 1]) for place in places
            ]
        for place in places:
            member, head = divmod(place, ratio)
            at = chunk * ratio + head
            decay_rows, decay_cols = decays[member]
            col = decay_cols[:, at : at + 1]
            fading = jnp.exp(jnp.minimum(col - decay_rows[at : at + 1], 0.0))
            weights = jnp.where(row_ids >= col_ids, scores[member] * fading, 0.0)
            scaled = queries[member] * jnp.exp(col)
            wy = wy_ref[place, rows]
            if chunk == 0:
                whole = mm(weights, wy)
                linear = scaled - whole[:, :HD]
                local = whole[:, HD:]
            else:
                gone = removed[place]
                left = jnp.concatenate([scaled, weights], axis=1)
                rest = jnp.concatenate(
                    [-gone[:, :HD], wy[:, HD:].astype(F32) - gone[:, HD:]], axis=1
                ).astype(BF)
                whole = mm(
                    left, jnp.concatenate([starts_ref[place, chunk - 1], rest], axis=0)
                )
                linear = whole[:, :HD]
                local = whole[:, HD:]
            parts_out[place, rows, :HD] = linear.astype(BF)
            parts_out[place, rows, HD:] = local.astype(BF)


def normed_heads(heads, swap, parts_ref, kept_ref, got_ref, gate_ref, normed_ref):
    half = heads // 2
    for head in range(heads):
        lanes = slice(head * HD, (head + 1) * HD)
        kept, got = kept_ref[head % half], got_ref[head % half]
        state = jnp.where(swap, got, kept) if head < half else jnp.where(swap, kept, got)
        attended = parts_ref[head, :, HD:].astype(F32) + mm(parts_ref[head, :, :HD], state)
        spread = lax.rsqrt(jnp.mean(attended * attended, axis=-1, keepdims=True) + 1e-06)
        normed_ref[:, lanes] = (
            attended * spread * silu(gate_ref[:, lanes].astype(F32))
        ).astype(BF)


def norm_kernel(heads, plan_ref, parts_ref, kept_ref, got_ref, gate_ref, normed_ref):
    normed_heads(heads, plan_ref[0] != 0, parts_ref, kept_ref, got_ref, gate_ref, normed_ref)


def far_kernel(
    heads,
    plan_ref,
    parts_hbm,
    kept_ref,
    got_ref,
    gate_ref,
    weight_hbm,
    out_ref,
    normed_ref,
    parts,
    weight,
    sems,
):
    pieces, depth, width = weight.shape
    length = parts.shape[1]
    rows = pl.ds(pl.multiple_of(plan_ref[1] * length, length), length)
    inward = pltpu.make_async_copy(parts_hbm.at[:, rows], parts, sems.at[pieces])
    copies = [
        pltpu.make_async_copy(
            weight_hbm.at[pl.ds(at * depth, depth), pl.ds(0, width)], weight.at[at], sems.at[at]
        )
        for at in range(pieces)
    ]
    for copy in [inward] + copies:
        copy.start()
    inward.wait()
    normed_heads(
        heads, plan_ref[0] != 0, parts, kept_ref, got_ref, gate_ref.at[rows], normed_ref
    )
    total = None
    for at, copy in enumerate(copies):
        copy.wait()
        part = jnp.dot(
            normed_ref[:, at * depth : (at + 1) * depth],
            weight[at],
            preferred_element_type=F32,
        )
        total = part if total is None else total + part
    out_ref[...] = total.astype(BF)


def far_rows(plan, parts, kept, got, gate_in, w_out, length, width):
    heads = parts.shape[0]
    features = w_out.shape[0]
    pieces = 4
    hbm = pl.BlockSpec(memory_space=pltpu.HBM)
    return pl.pallas_call(
        functools.partial(far_kernel, heads),
        in_specs=[SCALAR, hbm, WHOLE, WHOLE, WHOLE, hbm],
        out_specs=[WHOLE, WHOLE],
        out_shape=[
            jax.ShapeDtypeStruct((length, width), BF),
            jax.ShapeDtypeStruct((length, features), BF),
        ],
        scratch_shapes=[
            pltpu.VMEM((heads, length, 2 * HD), BF),
            pltpu.VMEM((pieces, features // pieces, width), BF),
            pltpu.SemaphoreType.DMA((pieces + 1,)),
        ],
        compiler_params=pltpu.CompilerParams(vmem_limit_bytes=20 << 20),
        name="far",
    )(plan, in_hbm(parts), kept, got, gate_in, w_out)


def normed_rows(first, count, plan, parts, kept, got, gate_in, length):
    heads = parts.shape[0]
    return pl.pallas_call(
        functools.partial(norm_kernel, heads),
        grid_spec=pltpu.PrefetchScalarGridSpec(
            num_scalar_prefetch=1,
            grid=(count,),
            in_specs=[
                pl.BlockSpec((heads, length, 2 * HD), lambda c, plan: (0, plan[1 + first + c], 0)),
                WHOLE,
                WHOLE,
                pl.BlockSpec((length, heads * HD), lambda c, plan: (plan[1 + first + c], 0)),
            ],
            out_specs=pl.BlockSpec((length, heads * HD), lambda c, plan: (c, 0)),
        ),
        out_shape=jax.ShapeDtypeStruct((count * length, heads * HD), BF),
        compiler_params=pltpu.CompilerParams(vmem_limit_bytes=16 << 20),
        cost_estimate=cost(
            heads * count * length, heads * count * length * HD, 8 * heads * count * length * HD
        ),
        name="normed",
    )(plan, in_hbm(parts), kept, got, gate_in)


def exchanged(value, axis, bit):
    count = lax.axis_size(axis)
    return lax.ppermute(value, axis, [(source, source ^ bit) for source in range(count)])


def after(later, earlier):
    moved = jnp.einsum(
        "hij,hjf->hif", later[..., :HD].astype(BF), earlier.astype(BF), preferred_element_type=F32
    )
    if earlier.shape[-1] == HD:
        return moved + later[..., HD:].astype(F32)
    in_state = lax.broadcasted_iota(jnp.int32, later.shape, 2) >= HD
    return moved + jnp.where(in_state, later.astype(F32), 0.0)


def incoming_state(total, axis, covers):
    early, late = covers
    count = lax.axis_size(axis)
    index = lax.axis_index(axis)
    odd = (index & 1) != 0
    half = total.shape[0] // 2
    mine = jnp.where(odd, total[half:], total[:half])
    other = exchanged(jnp.where(odd, total[:half], total[half:]), axis, 1)
    first = jnp.where(odd, other, mine)
    second = jnp.where(odd, mine, other)
    total = after(second, first).astype(BF)
    eye = jnp.broadcast_to(jnp.eye(HD, dtype=BF), (half, HD, HD))
    before = jnp.concatenate([eye, jnp.zeros_like(eye)], axis=-1)
    bit = 2
    while 2 * bit < count:
        high = (index & bit) != 0
        other = exchanged(total, axis, bit)
        if bit == 2:
            other, early = lax.optimization_barrier((other, early))
        lower, upper = jnp.where(high, other, total), jnp.where(high, total, other)
        if 4 * bit < count:
            total = after(upper, lower).astype(BF)
        else:
            total = after(upper, lower[..., HD:]).astype(BF)
        other, _ = lax.optimization_barrier((other, total))
        if bit == 2:
            before = jnp.where(high, other, before)
        else:
            before = jnp.where(high, after(before, other).astype(BF), before)
        bit *= 2
    high = (index & bit) != 0
    state = exchanged(total[..., -HD:], axis, bit)
    reach = jnp.where(high, before[..., :HD], jnp.zeros((), BF))
    before = jnp.concatenate([reach, before[..., HD:]], axis=-1)
    passed = after(first, before).astype(BF)
    keep, send = jnp.where(odd, passed, before), jnp.where(odd, before, passed)
    late = late(early)
    state, keep, send, late = lax.optimization_barrier((state, keep, send, late))
    got = exchanged(after(send, state).astype(BF), axis, 1)
    kept = after(keep, state).astype(BF)
    return kept, got, early, late


def summed(*values):
    total = values[0].astype(F32)
    for value in values[1:]:
        total = total + value.astype(F32)
    return total.astype(BF)


def line_sum(parts, axis):
    count = lax.axis_size(axis)
    index = lax.axis_index(axis)

    def take(at):
        return lax.dynamic_index_in_dim(parts, jnp.clip(at, 0, count - 1), 0, keepdims=False)

    up = down = None
    for step in range(count - 1):
        send_up = take(count - 1 - step + index)
        send_down = take(step - (count - 1 - index))
        if up is not None:
            send_up = summed(send_up, up)
            send_down = summed(send_down, down)
        up = lax.ppermute(send_up, axis, [(z, z + 1) for z in range(step + 1)])
        down = lax.ppermute(
            send_down, axis, [(count - 1 - z, count - 2 - z) for z in range(step + 1)]
        )
    return summed(take(index), up, down)


def mixed_rows(normed, w_out):
    return jnp.dot(normed, w_out, preferred_element_type=F32).astype(BF)


def swapped_sum(far, far_normed, w_out, rows_of, axis):
    width = far.shape[-1]
    early, late = slice(0, width), slice(width, w_out.shape[1])
    first_in = exchanged(far, axis, 1)
    far_normed, passed = lax.optimization_barrier((far_normed, rows_of(1, 1, far)))
    far_late = mixed_rows(far_normed, w_out)[:, late]
    later_in = exchanged(far_late, axis, 1)
    passed, _ = lax.optimization_barrier((passed, far_late))
    passed = mixed_rows(passed, w_out)
    paired = summed(passed[:, early], first_in)
    first = exchanged(paired, axis, 2)
    rest = mixed_rows(rows_of(2, 2, paired), w_out).reshape(2, -1, w_out.shape[1])
    later_in, first = lax.optimization_barrier((later_in, first))
    later = exchanged(summed(passed[:, late], later_in), axis, 2)
    near = exchanged(rest[0], axis, 1)
    own = rest[1]
    return jnp.concatenate(
        [
            summed(own[:, early], near[:, early], first),
            summed(own[:, late], near[:, late], later),
        ],
        axis=-1,
    )


def shards(
    inputs,
    w_query,
    w_key,
    w_value,
    w_gate_out,
    conv_query,
    conv_key,
    conv_value,
    decay_log,
    write_rate,
    w_out,
):
    def project(weights, earlier=None):
        tokens = inputs
        if earlier is not None:
            tokens, _ = lax.optimization_barrier((inputs, earlier))
        return jnp.dot(tokens, weights, preferred_element_type=F32).astype(BF)

    proj_key = project(w_key)
    proj_value = project(w_value)
    proj_query = project(w_query, (proj_key, proj_value))
    rows = inputs.shape[0]
    key_width = proj_key.shape[1]
    key_heads = key_width // HD
    heads = proj_value.shape[1] // HD
    ratio = heads // key_heads
    chunks = rows // CHUNK
    tails = jnp.concatenate(
        [proj_value[-RIM:], proj_key[-RIM:], proj_query[-RIM:]], axis=1
    )
    count = lax.axis_size("ctx")
    rims = lax.ppermute(tails, "ctx", [(at, (at + 1) % count) for at in range(count)])
    place_ctx = lax.axis_index("ctx").reshape(1)

    group = 2 if key_heads % 2 == 0 else 1

    def cols(length, width, start=0):
        return pl.BlockSpec((length, group * width), lambda h: (0, h + start // (group * width)))

    gate_spec = pl.BlockSpec((heads, rows), lambda h: (0, 0))
    wy_spec = pl.BlockSpec((group * ratio, rows, 2 * HD), lambda h: (h, 0, 0))
    starts_spec = pl.BlockSpec((group * ratio, chunks - 1, HD, 2 * HD), lambda h: (h, 0, 0, 0))
    taps_len = conv_key.shape[0]
    keys, wy, starts, total = pl.pallas_call(
        functools.partial(local_kernel, group, ratio, chunks),
        grid=(key_heads // group,),
        in_specs=[
            SCALAR,
            cols(rows, HD),
            cols(rows, ratio * HD),
            cols(RIM, HD, heads * HD),
            cols(RIM, ratio * HD),
            cols(taps_len, HD),
            cols(taps_len, ratio * HD),
            gate_spec,
            gate_spec,
        ],
        out_specs=[
            cols(rows, HD),
            wy_spec,
            starts_spec,
            pl.BlockSpec((group * ratio, HD, 2 * HD), lambda h: (h, 0, 0)),
        ],
        out_shape=[
            pltpu.HBM((rows, key_width), BF),
            pltpu.HBM((heads, rows, 2 * HD), BF),
            pltpu.HBM((heads, chunks - 1, HD, 2 * HD), BF),
            jax.ShapeDtypeStruct((heads, HD, 2 * HD), BF),
        ],
        scratch_shapes=[
            pltpu.VMEM((rows + 8, group * HD), F32),
            pltpu.VMEM((rows + 8, group * ratio * HD), F32),
        ],
        compiler_params=pltpu.CompilerParams(vmem_limit_bytes=32 << 20),
        cost_estimate=cost(16 * heads * rows, 4 * heads * rows * HD, 12 * heads * rows * HD),
        name="local",
    )(place_ctx, in_hbm(proj_key), in_hbm(proj_value), rims, rims, conv_key, conv_value, decay_log, write_rate)
    parts = pl.pallas_call(
        functools.partial(output_kernel, group, ratio, chunks),
        grid=(key_heads // group,),
        in_specs=[
            SCALAR,
            cols(rows, HD),
            cols(RIM, HD, key_width + heads * HD),
            cols(taps_len, HD),
            cols(rows, HD),
            wy_spec,
            starts_spec,
            gate_spec,
        ],
        out_specs=wy_spec,
        out_shape=pltpu.HBM((heads, rows, 2 * HD), BF),
        scratch_shapes=[pltpu.VMEM((rows + 8, group * HD), F32)],
        compiler_params=pltpu.CompilerParams(vmem_limit_bytes=24 << 20),
        cost_estimate=cost(8 * heads * rows, 2 * heads * rows * HD, 12 * heads * rows * HD),
        name="outputs",
    )(place_ctx, in_hbm(proj_query), rims, conv_query, in_hbm(keys), in_hbm(wy), in_hbm(starts), decay_log)
    kept, got, parts, gate_in = incoming_state(total, "ctx", (parts, functools.partial(project, w_gate_out)))
    spread = lax.axis_size("head")
    place = lax.axis_index("head")
    length = rows // spread
    swap = lax.axis_index("ctx") & 1
    if spread == 4:
        order = [place ^ 3, place ^ 2, place ^ 1, place]
    else:
        order = list(range(spread))
    plan = jnp.stack([jnp.int32(at) for at in [swap] + order])

    def rows_of(first, amount, earlier):
        steps = plan
        if earlier is not None:
            steps, _ = lax.optimization_barrier((plan, earlier))
        return normed_rows(first, amount, steps, parts, kept, got, gate_in, length)

    if spread == 4:
        far, far_normed = far_rows(
            plan, parts, kept, got, gate_in, w_out, length, 3 * w_out.shape[1] // 8
        )
        return swapped_sum(far, far_normed, w_out, rows_of, "head")
    whole = mixed_rows(rows_of(0, spread, None), w_out)
    return line_sum(whole.reshape(spread, length, w_out.shape[1]), "head")


def solution(mesh):
    return jax.shard_map(
        shards,
        mesh=mesh,
        in_specs=(
            P("ctx", None),
            P(None, "head"),
            P(None, "head"),
            P(None, "head"),
            P(None, "head"),
            P(None, "head"),
            P(None, "head"),
            P(None, "head"),
            P("head", "ctx"),
            P("head", "ctx"),
            P("head", None),
        ),
        out_specs=P(("ctx", "head"), None),
        check_vma=False,
    )
```

```python
import functools

import jax
import jax.numpy as jnp
from jax import lax
from jax.experimental import pallas as pl
from jax.experimental.pallas import tpu as pltpu
from jax.sharding import PartitionSpec as P

HD = 128
CHUNK = 128
RIM = 8
BF = jnp.bfloat16
F32 = jnp.float32
EXACT = lax.Precision.HIGHEST
SCALAR = pl.BlockSpec(memory_space=pltpu.SMEM)
WHOLE = pl.BlockSpec(memory_space=pltpu.VMEM)


def cost(matmul_rows, exps, size):
    return pl.CostEstimate(
        flops=2 * HD * HD * matmul_rows, transcendentals=exps, bytes_accessed=size
    )


def in_hbm(array):
    return pltpu.with_memory_space_constraint(array, pltpu.HBM)


def mm(left, right):
    return jnp.dot(left.astype(BF), right.astype(BF), preferred_element_type=F32)


def mm_nt(left, right):
    return lax.dot_general(
        left.astype(BF), right.astype(BF), (((1,), (1,)), ((), ())), preferred_element_type=F32
    )


def silu(values):
    return values / (1.0 + jnp.exp(-values))


def unit_rows(values, factor):
    return values * (lax.rsqrt(jnp.sum(values * values, axis=-1, keepdims=True) + 1e-06) * factor)


def stage_rows(stage, at_ref, rims_ref, rows_ref):
    stage[0:8] = jnp.where(at_ref[0] > 0, rims_ref[RIM - 8 : RIM].astype(F32), 0.0)
    stage[8:] = rows_ref[...].astype(F32)


def conv_chunk(stage, taps, chunk):
    taps_len = taps.shape[0]
    start = 8 - (taps_len - 1) + chunk * CHUNK
    total = taps[0:1] * stage[start : start + CHUNK]
    for offset in range(1, taps_len):
        total = total + taps[offset : offset + 1] * stage[start + offset : start + offset + CHUNK]
    return silu(total)


def grid_ids():
    row_ids = lax.broadcasted_iota(jnp.int32, (CHUNK, CHUNK), 0)
    col_ids = lax.broadcasted_iota(jnp.int32, (CHUNK, CHUNK), 1)
    return row_ids, col_ids


def cumulated(decay):
    row_ids, col_ids = grid_ids()
    lower = jnp.where(row_ids >= col_ids, 1.0, 0.0)
    as_rows = lax.dot_general(
        decay, lower, (((1,), (1,)), ((), ())), precision=EXACT, preferred_element_type=F32
    )
    return as_rows, as_rows.T


def head_rows(ref, ratio, chunks, group=1, member=0):
    start = (pl.program_id(0) * group + member) * ratio
    rows = [ref[pl.ds(start + head, 1), :] for head in range(ratio)]
    return jnp.concatenate(
        [
            row[:, chunk * CHUNK : (chunk + 1) * CHUNK]
            for chunk in range(chunks)
            for row in rows
        ],
        axis=0,
    )


def inverted(systems):
    row_ids, col_ids = grid_ids()
    same = row_ids // 2 == col_ids // 2
    eye = jnp.where(row_ids == col_ids, 1.0, 0.0)
    inverses = [eye - jnp.where(same, system, 0.0) for system in systems]
    size = 2
    while size < CHUNK:
        cross = (row_ids // (2 * size) == col_ids // (2 * size)) & (
            row_ids // size != col_ids // size
        )
        links = [jnp.where(cross, system, 0.0).astype(BF) for system in systems]
        halves = [inverse.astype(BF) for inverse in inverses]
        if size < 8:
            inner = [mm(link, half) for link, half in zip(links, halves)]
            outer = [mm(half, part) for half, part in zip(halves, inner)]
            inverses = [inverse - part for inverse, part in zip(inverses, outer)]
        else:
            starts = range(size, CHUNK, 2 * size)
            odd = [
                jnp.concatenate([inverse[s : s + size] for s in starts], axis=0)
                for inverse in inverses
            ]
            inner = [mm(part, link) for part, link in zip(odd, links)]
            outer = [mm(part, half) for part, half in zip(inner, halves)]
            odd = [part - update for part, update in zip(odd, outer)]
            inverses = [
                jnp.concatenate(
                    [
                        piece
                        for at, s in enumerate(starts)
                        for piece in (
                            inverse[s - size : s],
                            part[at * size : (at + 1) * size],
                        )
                    ],
                    axis=0,
                )
                for inverse, part in zip(inverses, odd)
            ]
        size *= 2
    return inverses


def local_kernel(
    group,
    ratio,
    chunks,
    at_ref,
    keys_ref,
    values_ref,
    rims_k_ref,
    rims_v_ref,
    taps_k_ref,
    taps_v_ref,
    decay_ref,
    write_ref,
    keys_out,
    wy_out,
    starts_out,
    map_out,
    stage_k,
    stage_v,
):
    row_ids, col_ids = grid_ids()
    eye = jnp.where(row_ids == col_ids, 1.0, 0.0)
    stage_rows(stage_k, at_ref, rims_k_ref, keys_ref)
    stage_rows(stage_v, at_ref, rims_v_ref, values_ref)
    taps_k = taps_k_ref[...]
    taps_v = taps_v_ref[...]
    decays = []
    writes = []
    for member in range(group):
        decays.append(cumulated(head_rows(decay_ref, ratio, chunks, group, member)))
        writes.append(head_rows(write_ref, ratio, chunks, group, member).T)
    keys = {}
    flipped = {}
    values = []
    inner = {}
    for chunk in range(chunks):
        rows = slice(chunk * CHUNK, (chunk + 1) * CHUNK)
        smoothed = conv_chunk(stage_k, taps_k, chunk)
        values.append(conv_chunk(stage_v, taps_v, chunk))
        for member in range(group):
            lanes = slice(member * HD, (member + 1) * HD)
            key = unit_rows(smoothed[:, lanes], 1.0)
            keys_out[rows, lanes] = key.astype(BF)
            keys[member, chunk] = key
            flipped[member, chunk] = key.T
            inner[member, chunk] = mm(key, flipped[member, chunk])
    units = [
        (member, head, chunk)
        for member in range(group)
        for head in range(ratio)
        for chunk in range(chunks)
    ]
    systems = []
    for member, head, chunk in units:
        at = chunk * ratio + head
        decay_rows, decay_cols = decays[member]
        fading = jnp.exp(
            jnp.minimum(decay_cols[:, at : at + 1] - decay_rows[at : at + 1], 0.0)
        )
        systems.append(
            jnp.where(
                row_ids > col_ids,
                writes[member][:, at : at + 1] * inner[member, chunk] * fading,
                0.0,
            )
        )
    inverses = inverted(systems)
    maps = {}
    for (member, head, chunk), inverse in zip(units, inverses):
        at = chunk * ratio + head
        place = member * ratio + head
        decay_rows, decay_cols = decays[member]
        col = decay_cols[:, at : at + 1]
        write = writes[member][:, at : at + 1]
        value = values[chunk][:, place * HD : (place + 1) * HD]
        right = jnp.concatenate(
            [keys[member, chunk] * (write * jnp.exp(col)), value * write], axis=1
        )
        solved = mm(inverse, right).astype(BF)
        wy_out[place, chunk * CHUNK : (chunk + 1) * CHUNK] = solved
        row = decay_rows[at : at + 1]
        end = row[:, CHUNK - 1 : CHUNK]
        maps[place, chunk] = (
            mm(flipped[member, chunk] * jnp.exp(end - row), solved),
            jnp.exp(end),
        )
    states = [None] * (group * ratio)
    for chunk in range(chunks):
        for place, state in enumerate(states):
            product, end = maps[place, chunk]
            removed, added = product[:, :HD], product[:, HD:]
            if state is None:
                states[place] = jnp.concatenate([eye * end - removed, added], axis=1)
            else:
                starts_out[place, chunk - 1] = state.astype(BF)
                moved = end * state - mm(removed, state)
                states[place] = jnp.concatenate([moved[:, :HD], moved[:, HD:] + added], axis=1)
    for place, state in enumerate(states):
        map_out[place] = state.astype(BF)


def output_kernel(
    group,
    ratio,
    chunks,
    at_ref,
    query_ref,
    rims_ref,
    taps_ref,
    keys_ref,
    wy_ref,
    starts_ref,
    decay_ref,
    parts_out,
    stage,
):
    row_ids, col_ids = grid_ids()
    stage_rows(stage, at_ref, rims_ref, query_ref)
    decays = [
        cumulated(head_rows(decay_ref, ratio, chunks, group, member)) for member in range(group)
    ]
    taps = taps_ref[...]
    for chunk in range(chunks):
        rows = slice(chunk * CHUNK, (chunk + 1) * CHUNK)
        smoothed = conv_chunk(stage, taps, chunk)
        places = range(group * ratio)
        queries, scores = [], []
        for member in range(group):
            lanes = slice(member * HD, (member + 1) * HD)
            queries.append(unit_rows(smoothed[:, lanes], HD ** (-0.5)))
            scores.append(mm_nt(queries[-1], keys_ref[rows, lanes]))
        if chunk > 0:
            removed = [
                mm(wy_ref[place, rows, :HD], starts_ref[place, chunk - 1]) for place in places
            ]
        for place in places:
            member, head = divmod(place, ratio)
            at = chunk * ratio + head
            decay_rows, decay_cols = decays[member]
            col = decay_cols[:, at : at + 1]
            fading = jnp.exp(jnp.minimum(col - decay_rows[at : at + 1], 0.0))
            weights = jnp.where(row_ids >= col_ids, scores[member] * fading, 0.0)
            scaled = queries[member] * jnp.exp(col)
            wy = wy_ref[place, rows]
            if chunk == 0:
                whole = mm(weights, wy)
                linear = scaled - whole[:, :HD]
                local = whole[:, HD:]
            else:
                gone = removed[place]
                left = jnp.concatenate([scaled, weights], axis=1)
                rest = jnp.concatenate(
                    [-gone[:, :HD], wy[:, HD:].astype(F32) - gone[:, HD:]], axis=1
                ).astype(BF)
                whole = mm(
                    left, jnp.concatenate([starts_ref[place, chunk - 1], rest], axis=0)
                )
                linear = whole[:, :HD]
                local = whole[:, HD:]
            parts_out[place, rows, :HD] = linear.astype(BF)
            parts_out[place, rows, HD:] = local.astype(BF)


def normed_heads(heads, swap, parts_ref, kept_ref, got_ref, gate_ref, normed_ref):
    half = heads // 2
    for head in range(heads):
        lanes = slice(head * HD, (head + 1) * HD)
        kept, got = kept_ref[head % half], got_ref[head % half]
        state = jnp.where(swap, got, kept) if head < half else jnp.where(swap, kept, got)
        attended = parts_ref[head, :, HD:].astype(F32) + mm(parts_ref[head, :, :HD], state)
        spread = lax.rsqrt(jnp.mean(attended * attended, axis=-1, keepdims=True) + 1e-06)
        normed_ref[:, lanes] = (
            attended * spread * silu(gate_ref[:, lanes].astype(F32))
        ).astype(BF)


def norm_kernel(heads, plan_ref, parts_ref, kept_ref, got_ref, gate_ref, normed_ref):
    normed_heads(heads, plan_ref[0] != 0, parts_ref, kept_ref, got_ref, gate_ref, normed_ref)


def far_kernel(
    heads,
    plan_ref,
    parts_hbm,
    kept_ref,
    got_ref,
    gate_ref,
    weight_hbm,
    out_ref,
    normed_ref,
    parts,
    weight,
    sems,
):
    pieces, depth, width = weight.shape
    length = parts.shape[1]
    rows = pl.ds(pl.multiple_of(plan_ref[1] * length, length), length)
    inward = pltpu.make_async_copy(parts_hbm.at[:, rows], parts, sems.at[pieces])
    copies = [
        pltpu.make_async_copy(
            weight_hbm.at[pl.ds(at * depth, depth), pl.ds(0, width)], weight.at[at], sems.at[at]
        )
        for at in range(pieces)
    ]
    for copy in [inward] + copies:
        copy.start()
    inward.wait()
    normed_heads(
        heads, plan_ref[0] != 0, parts, kept_ref, got_ref, gate_ref.at[rows], normed_ref
    )
    total = None
    for at, copy in enumerate(copies):
        copy.wait()
        part = jnp.dot(
            normed_ref[:, at * depth : (at + 1) * depth],
            weight[at],
            preferred_element_type=F32,
        )
        total = part if total is None else total + part
    out_ref[...] = total.astype(BF)


def far_rows(plan, parts, kept, got, gate_in, w_out, length, width):
    heads = parts.shape[0]
    features = w_out.shape[0]
    pieces = 4
    hbm = pl.BlockSpec(memory_space=pltpu.HBM)
    return pl.pallas_call(
        functools.partial(far_kernel, heads),
        in_specs=[SCALAR, hbm, WHOLE, WHOLE, WHOLE, hbm],
        out_specs=[WHOLE, WHOLE],
        out_shape=[
            jax.ShapeDtypeStruct((length, width), BF),
            jax.ShapeDtypeStruct((length, features), BF),
        ],
        scratch_shapes=[
            pltpu.VMEM((heads, length, 2 * HD), BF),
            pltpu.VMEM((pieces, features // pieces, width), BF),
            pltpu.SemaphoreType.DMA((pieces + 1,)),
        ],
        compiler_params=pltpu.CompilerParams(vmem_limit_bytes=20 << 20),
        name="far",
    )(plan, in_hbm(parts), kept, got, gate_in, w_out)


def normed_rows(first, count, plan, parts, kept, got, gate_in, length):
    heads = parts.shape[0]
    return pl.pallas_call(
        functools.partial(norm_kernel, heads),
        grid_spec=pltpu.PrefetchScalarGridSpec(
            num_scalar_prefetch=1,
            grid=(count,),
            in_specs=[
                pl.BlockSpec((heads, length, 2 * HD), lambda c, plan: (0, plan[1 + first + c], 0)),
                WHOLE,
                WHOLE,
                pl.BlockSpec((length, heads * HD), lambda c, plan: (plan[1 + first + c], 0)),
            ],
            out_specs=pl.BlockSpec((length, heads * HD), lambda c, plan: (c, 0)),
        ),
        out_shape=jax.ShapeDtypeStruct((count * length, heads * HD), BF),
        compiler_params=pltpu.CompilerParams(vmem_limit_bytes=16 << 20),
        cost_estimate=cost(
            heads * count * length, heads * count * length * HD, 8 * heads * count * length * HD
        ),
        name="normed",
    )(plan, in_hbm(parts), kept, got, gate_in)


def exchanged(value, axis, bit):
    count = lax.axis_size(axis)
    return lax.ppermute(value, axis, [(source, source ^ bit) for source in range(count)])


def after(later, earlier):
    moved = jnp.einsum(
        "hij,hjf->hif", later[..., :HD].astype(BF), earlier.astype(BF), preferred_element_type=F32
    )
    if earlier.shape[-1] == HD:
        return moved + later[..., HD:].astype(F32)
    in_state = lax.broadcasted_iota(jnp.int32, later.shape, 2) >= HD
    return moved + jnp.where(in_state, later.astype(F32), 0.0)


def incoming_state(total, axis, covers):
    early, late = covers
    count = lax.axis_size(axis)
    index = lax.axis_index(axis)
    odd = (index & 1) != 0
    half = total.shape[0] // 2
    mine = jnp.where(odd, total[half:], total[:half])
    other = exchanged(jnp.where(odd, total[:half], total[half:]), axis, 1)
    first = jnp.where(odd, other, mine)
    second = jnp.where(odd, mine, other)
    total = after(second, first).astype(BF)
    eye = jnp.broadcast_to(jnp.eye(HD, dtype=BF), (half, HD, HD))
    before = jnp.concatenate([eye, jnp.zeros_like(eye)], axis=-1)
    bit = 2
    while 2 * bit < count:
        high = (index & bit) != 0
        other = exchanged(total, axis, bit)
        if bit == 2:
            other, early = lax.optimization_barrier((other, early))
        lower, upper = jnp.where(high, other, total), jnp.where(high, total, other)
        if 4 * bit < count:
            total = after(upper, lower).astype(BF)
        else:
            total = after(upper, lower[..., HD:]).astype(BF)
        other, _ = lax.optimization_barrier((other, total))
        if bit == 2:
            before = jnp.where(high, other, before)
        else:
            before = jnp.where(high, after(before, other).astype(BF), before)
        bit *= 2
    high = (index & bit) != 0
    state = exchanged(total[..., -HD:], axis, bit)
    reach = jnp.where(high, before[..., :HD], jnp.zeros((), BF))
    before = jnp.concatenate([reach, before[..., HD:]], axis=-1)
    passed = after(first, before).astype(BF)
    keep, send = jnp.where(odd, passed, before), jnp.where(odd, before, passed)
    late = late(early)
    state, keep, send, late = lax.optimization_barrier((state, keep, send, late))
    got = exchanged(after(send, state).astype(BF), axis, 1)
    kept = after(keep, state).astype(BF)
    return kept, got, early, late


def summed(*values):
    total = values[0].astype(F32)
    for value in values[1:]:
        total = total + value.astype(F32)
    return total.astype(BF)


def line_sum(parts, axis):
    count = lax.axis_size(axis)
    index = lax.axis_index(axis)

    def take(at):
        return lax.dynamic_index_in_dim(parts, jnp.clip(at, 0, count - 1), 0, keepdims=False)

    up = down = None
    for step in range(count - 1):
        send_up = take(count - 1 - step + index)
        send_down = take(step - (count - 1 - index))
        if up is not None:
            send_up = summed(send_up, up)
            send_down = summed(send_down, down)
        up = lax.ppermute(send_up, axis, [(z, z + 1) for z in range(step + 1)])
        down = lax.ppermute(
            send_down, axis, [(count - 1 - z, count - 2 - z) for z in range(step + 1)]
        )
    return summed(take(index), up, down)


def mixed_rows(normed, w_out):
    return jnp.dot(normed, w_out, preferred_element_type=F32).astype(BF)


def swapped_sum(far, far_normed, w_out, rows_of, axis):
    width = far.shape[-1]
    early, late = slice(0, width), slice(width, w_out.shape[1])
    first_in = exchanged(far, axis, 1)
    far_normed, passed = lax.optimization_barrier((far_normed, rows_of(1, 1, far)))
    far_late = mixed_rows(far_normed, w_out)[:, late]
    later_in = exchanged(far_late, axis, 1)
    passed, _ = lax.optimization_barrier((passed, far_late))
    passed = mixed_rows(passed, w_out)
    paired = summed(passed[:, early], first_in)
    first = exchanged(paired, axis, 2)
    rest = mixed_rows(rows_of(2, 2, paired), w_out).reshape(2, -1, w_out.shape[1])
    later_in, first = lax.optimization_barrier((later_in, first))
    later = summed(passed[:, late], later_in)
    near_early = exchanged(rest[0][:, early], axis, 1)
    near_rows, _ = lax.optimization_barrier((rest[0][:, late], later))
    later = exchanged(later, axis, 2)
    near_late = exchanged(near_rows, axis, 1)
    own = rest[1]
    return jnp.concatenate(
        [
            summed(own[:, early], near_early, first),
            summed(own[:, late], near_late, later),
        ],
        axis=-1,
    )


def shards(
    inputs,
    w_query,
    w_key,
    w_value,
    w_gate_out,
    conv_query,
    conv_key,
    conv_value,
    decay_log,
    write_rate,
    w_out,
):
    def project(weights, earlier=None):
        tokens = inputs
        if earlier is not None:
            tokens, _ = lax.optimization_barrier((inputs, earlier))
        return jnp.dot(tokens, weights, preferred_element_type=F32).astype(BF)

    proj_key = project(w_key)
    proj_value = project(w_value)
    proj_query = project(w_query, (proj_key, proj_value))
    rows = inputs.shape[0]
    key_width = proj_key.shape[1]
    key_heads = key_width // HD
    heads = proj_value.shape[1] // HD
    ratio = heads // key_heads
    chunks = rows // CHUNK
    tails = jnp.concatenate(
        [proj_value[-RIM:], proj_key[-RIM:], proj_query[-RIM:]], axis=1
    )
    count = lax.axis_size("ctx")
    rims = lax.ppermute(tails, "ctx", [(at, (at + 1) % count) for at in range(count)])
    place_ctx = lax.axis_index("ctx").reshape(1)

    group = 2 if key_heads % 2 == 0 else 1

    def cols(length, width, start=0):
        return pl.BlockSpec((length, group * width), lambda h: (0, h + start // (group * width)))

    gate_spec = pl.BlockSpec((heads, rows), lambda h: (0, 0))
    wy_spec = pl.BlockSpec((group * ratio, rows, 2 * HD), lambda h: (h, 0, 0))
    starts_spec = pl.BlockSpec((group * ratio, chunks - 1, HD, 2 * HD), lambda h: (h, 0, 0, 0))
    taps_len = conv_key.shape[0]
    keys, wy, starts, total = pl.pallas_call(
        functools.partial(local_kernel, group, ratio, chunks),
        grid=(key_heads // group,),
        in_specs=[
            SCALAR,
            cols(rows, HD),
            cols(rows, ratio * HD),
            cols(RIM, HD, heads * HD),
            cols(RIM, ratio * HD),
            cols(taps_len, HD),
            cols(taps_len, ratio * HD),
            gate_spec,
            gate_spec,
        ],
        out_specs=[
            cols(rows, HD),
            wy_spec,
            starts_spec,
            pl.BlockSpec((group * ratio, HD, 2 * HD), lambda h: (h, 0, 0)),
        ],
        out_shape=[
            pltpu.HBM((rows, key_width), BF),
            pltpu.HBM((heads, rows, 2 * HD), BF),
            pltpu.HBM((heads, chunks - 1, HD, 2 * HD), BF),
            jax.ShapeDtypeStruct((heads, HD, 2 * HD), BF),
        ],
        scratch_shapes=[
            pltpu.VMEM((rows + 8, group * HD), F32),
            pltpu.VMEM((rows + 8, group * ratio * HD), F32),
        ],
        compiler_params=pltpu.CompilerParams(vmem_limit_bytes=32 << 20),
        cost_estimate=cost(16 * heads * rows, 4 * heads * rows * HD, 12 * heads * rows * HD),
        name="local",
    )(place_ctx, in_hbm(proj_key), in_hbm(proj_value), rims, rims, conv_key, conv_value, decay_log, write_rate)
    parts = pl.pallas_call(
        functools.partial(output_kernel, group, ratio, chunks),
        grid=(key_heads // group,),
        in_specs=[
            SCALAR,
            cols(rows, HD),
            cols(RIM, HD, key_width + heads * HD),
            cols(taps_len, HD),
            cols(rows, HD),
            wy_spec,
            starts_spec,
            gate_spec,
        ],
        out_specs=wy_spec,
        out_shape=pltpu.HBM((heads, rows, 2 * HD), BF),
        scratch_shapes=[pltpu.VMEM((rows + 8, group * HD), F32)],
        compiler_params=pltpu.CompilerParams(vmem_limit_bytes=24 << 20),
        cost_estimate=cost(8 * heads * rows, 2 * heads * rows * HD, 12 * heads * rows * HD),
        name="outputs",
    )(place_ctx, in_hbm(proj_query), rims, conv_query, in_hbm(keys), in_hbm(wy), in_hbm(starts), decay_log)
    kept, got, parts, gate_in = incoming_state(total, "ctx", (parts, functools.partial(project, w_gate_out)))
    spread = lax.axis_size("head")
    place = lax.axis_index("head")
    length = rows // spread
    swap = lax.axis_index("ctx") & 1
    if spread == 4:
        order = [place ^ 3, place ^ 2, place ^ 1, place]
    else:
        order = list(range(spread))
    plan = jnp.stack([jnp.int32(at) for at in [swap] + order])

    def rows_of(first, amount, earlier):
        steps = plan
        if earlier is not None:
            steps, _ = lax.optimization_barrier((plan, earlier))
        return normed_rows(first, amount, steps, parts, kept, got, gate_in, length)

    if spread == 4:
        far, far_normed = far_rows(
            plan, parts, kept, got, gate_in, w_out, length, 3 * w_out.shape[1] // 8
        )
        return swapped_sum(far, far_normed, w_out, rows_of, "head")
    whole = mixed_rows(rows_of(0, spread, None), w_out)
    return line_sum(whole.reshape(spread, length, w_out.shape[1]), "head")


def solution(mesh):
    return jax.shard_map(
        shards,
        mesh=mesh,
        in_specs=(
            P("ctx", None),
            P(None, "head"),
            P(None, "head"),
            P(None, "head"),
            P(None, "head"),
            P(None, "head"),
            P(None, "head"),
            P(None, "head"),
            P("head", "ctx"),
            P("head", "ctx"),
            P("head", None),
        ),
        out_specs=P(("ctx", "head"), None),
        check_vma=False,
    )
```
